512 devices in a mesh: dp: 32 (over y_lo, z), mp: 16 (over x, y_hi, core).
Axes of the slice: x: 4, y: 4 (y_hi: 2, y_lo: 2; y = y_hi * 2 + y_lo), z: 16, core: 2. Of those that a mesh axis runs over, the one named last changes fastest.
Arguments:
- hidden: bfloat16 [8192, 8192], P('dp', 'mp'), may hold values from -6 to 6
- target_gain: float32 [8192], replicated, may hold values from 0.1 to 1.9
- target_weight: bfloat16 [2048, 8192], P('mp'), may hold values from -0.0625 to 0.0625
- draft_gain: float32 [8192], P('mp'), may hold values from 0.1 to 1.9
- draft_weight: bfloat16 [2048, 8192], P('dp', 'mp'), may hold values from -0.0625 to 0.0625
- logits: bfloat16 [8192, 32000], P('dp', 'mp'), may hold values from -40 to 300
- seq_lens: int32 [32, 2], P('dp'), may hold values from 32 to 128, as said below
- tool_mask: int32 [8192], P('dp'), may hold values 0 or 1
- owners: int32 [8192, 1], P('dp'), may hold values from 0 to 31; in each aligned block of 256 rows (0 to 255, 256 to 511, ...) at most 10 rows name the same one
Outputs:
- grad_weight: float32 [2048, 8192], P('dp', 'mp')
- grad_gain: float32 [8192], P('mp')
- slot_loss: float32 [10240], P('dp')
The draws below stay inside these ranges and needn't reach their ends.
Inputs may be any that keep to these rules, and one draw needn't show every extreme that they name: `owners`: in the rows of one index of dp at most 10 name the same owner, a bound that some block reaches. `seq_lens`: in each index of dp some sequence has length exactly 128.
All inputs are finite; a program needn't handle non-finite values. No bound on the sum of `tool_mask` on one device may be relied on, other than what follows from the above.
Results may differ from the reference program's by a relative error of at most 0.0085.
Values may be sent and summed in bfloat16 or wider, within the bound.
No kernel may reach another device: no remote copies, remote signals or barrier semaphores. Data moves between devices by JAX's collectives and lax.ppermute only.
A program may use at most 64 MiB of HBM per device.

```python
import math
import jax
import jax.numpy as jnp
import numpy as np
from jax import lax

D = 8192
VOCAB = 32000
LEN = 128
SEQS = 2
KVW = 2048
TOK = 256
GROUPS = 32
TOKENS = 8192
CAP = 10
N_DP = 32


def draw_logits(key, part):
    keys = jax.random.split(key, 2)
    spread = jnp.exp(jax.random.uniform(keys[0], (TOKENS, 1), minval=0.0, maxval=math.log(4.0)))
    values = jnp.clip(3.0 * spread * jax.random.normal(keys[1], (TOKENS, VOCAB)), -40.0, 40.0)
    return values.astype(jnp.bfloat16)


def draw_seq_lens(key, part):
    keys = jax.random.split(jax.random.fold_in(key, 17), 2)
    lengths = jax.random.randint(keys[0], (GROUPS, SEQS), LEN // 4, LEN + 1)
    longest = jax.random.randint(keys[1], (GROUPS, 1), 0, SEQS)
    column = jnp.arange(SEQS, dtype=jnp.int32)[None, :]
    return jnp.where(column == longest, LEN, lengths).astype(jnp.int32)


def place_ends(array, key, least, high):
    dims = array.shape
    spot = [jax.random.randint(jax.random.fold_in(key, axis), (), 0, dims[axis]) for axis in range(len(dims))]
    array = array.at[tuple(spot)].set(least)
    longest = dims.index(max(dims))
    spot[longest] = (spot[longest] + 1) % dims[longest]
    return array.at[tuple(spot)].set(high)


def block_levels(own_key, extent, pieces, least, largest):
    def one(dim, parts):
        heights = jax.random.uniform(jax.random.fold_in(jax.random.fold_in(own_key, 6), dim), (parts,), jnp.float32, least / len(pieces), largest / len(pieces))
        return jnp.repeat(jnp.exp(heights), extent[dim] // parts).reshape((-1,) + (1,) * (len(extent) - dim - 1))

    loudness = one(*pieces[0])
    for cut in pieces[1:]:
        loudness = loudness * one(*cut)
    return loudness


def shared_out(rng, own, number, rows, count, top, bound, lean):
    ranking = jax.random.permutation(rng, count)
    crowded, ordinary = load_shares(count, rows * top, bound, lean, True), load_shares(count, rows * top, bound, lean, False)
    places = jnp.arange(count)

    def named(sizes, rotation):
        used = int((sizes > 0).sum())
        fixed = max(1, used // 4)
        moved = fixed + (places - fixed + rotation * (used - fixed)) % max(1, count - fixed)
        return jnp.zeros((count,), jnp.int32).at[ranking[jnp.where(places < fixed, places, moved)]].set(jnp.asarray(sizes, jnp.int32))

    sizes = jnp.where(number % 4 == 0, named(crowded, number // 4), named(ordinary, number - number // 4 - 1))
    mixed = jax.random.permutation(jax.random.fold_in(own, 3), count)
    source_of, sink = mixed[0:count // 2 * 2:2], mixed[1:count // 2 * 2:2]
    slack = jnp.minimum(sizes[source_of] - 1, bound - sizes[sink]) // 2
    slack = jnp.where((source_of == ranking[0]) | (sink == ranking[0]) | (sizes[sink] == 0), 0, jnp.maximum(slack, 0))
    moved = jax.random.randint(jax.random.fold_in(own, 4), (count // 2,), 0, 1 << 20) % (slack + 1)
    sizes = sizes.at[source_of].add(-moved).at[sink].add(moved)
    items = jnp.searchsorted(jnp.cumsum(sizes), jnp.arange(rows * top), side="right").astype(jnp.int32)
    grid = items.reshape(top, rows).T
    grid = grid[jax.random.permutation(jax.random.fold_in(own, 1), rows)]
    rotation = jax.random.randint(jax.random.fold_in(own, 2), (rows, 1), 0, top)
    return jnp.take_along_axis(grid, (jnp.arange(top)[None, :] + rotation) % top, axis=1)


def load_shares(count, total, most, lean, full):
    portions = [(1 << 20) // math.isqrt(standing ** lean) + 1 for standing in range(1, count + 1)]
    largest = most if full else min(most, max(-(-total // count), total * portions[0] // sum(portions)))
    least = 1 if total - largest >= count - 1 else 0
    counts, surplus = [largest] + [least] * (count - 1), total - largest - least * (count - 1)
    while surplus > 0:
        free = [i for i in range(1, count) if counts[i] < largest] or [i for i in range(1, count) if counts[i] < most]
        mass, remaining = sum([portions[i] for i in free]), surplus
        for i in free:
            more = min(most - counts[i], max(1, remaining * portions[i] // mass), surplus)
            counts[i] = counts[i] + more
            surplus = surplus - more
    return np.array(counts)


def centred(rng, shape, scale, limit, cuts=(), kind=jnp.bfloat16):
    array = jax.random.normal(rng, shape, jnp.float32) * scale
    if len(cuts) > 0:
        array = block_levels(rng, shape, cuts, -0.22, 0.18) * array
    return jnp.clip(array, min=-limit, max=limit).astype(kind)


def setup_inputs(seed: int = 0) -> dict:
    streams_of = jax.random.split(jax.random.key(seed), 10)
    hidden = centred(streams_of[0], (TOKENS, D), 1.0, 6.0, ((0, 32), (1, 16)))
    target_gain = jnp.clip(1.0 + 0.18 * jax.random.normal(streams_of[1], (D,), jnp.float32), 0.1, 1.9)
    target_weight = centred(streams_of[2], (KVW, D), D ** -0.5, 0.0625, ((0, 16),))
    draft_gain = jnp.clip(1.0 + 0.18 * jax.random.normal(streams_of[3], (D,), jnp.float32), 0.1, 1.9)
    draft_weight = centred(streams_of[4], (KVW, D), D ** -0.5, 0.0625, ((0, 32), (1, 16)))
    logits = draw_logits(jax.random.fold_in(streams_of[9], 71), 0)
    seq_lens = draw_seq_lens(jax.random.fold_in(streams_of[9], 71), 0)
    tool_mask = place_ends((jax.random.randint(streams_of[7], (TOKENS,), 0, 4) < 3).astype(jnp.int32), jax.random.fold_in(streams_of[7], 1), 0, 1)
    owners_keys = jax.random.split(jax.random.fold_in(streams_of[8], 1), TOKENS // TOK)
    owners_turns = jax.random.permutation(jax.random.fold_in(streams_of[8], 3), TOKENS // TOK)
    owners = jax.vmap(lambda own, number: shared_out(jax.random.fold_in(streams_of[8], 2), own, number, TOK, N_DP, 1, CAP, 2))(owners_keys, owners_turns).reshape((TOKENS, 1))
    return dict(hidden=hidden, target_gain=target_gain, target_weight=target_weight, draft_gain=draft_gain, draft_weight=draft_weight, logits=logits, seq_lens=seq_lens, tool_mask=tool_mask, owners=owners)


EPSILON = 1e-05

def row_entropy(block):
    values = block.astype(jnp.float32)
    highest = lax.optimization_barrier(jnp.max(values, axis=1))
    shifted = values - highest[:, None]
    expsum = jnp.exp(shifted)
    total = lax.optimization_barrier(jnp.sum(expsum, axis=1))
    moment = lax.optimization_barrier(jnp.sum(expsum * shifted, axis=1))
    return jnp.log(total) - moment / total

def reference(hidden, target_gain, target_weight, draft_gain, draft_weight, logits, seq_lens, tool_mask, owners):
    hidden_float = hidden.astype(jnp.float32)
    inverse = lax.rsqrt(lax.optimization_barrier(jnp.mean(hidden_float * hidden_float, axis=1)) + EPSILON)
    target_in = (hidden_float * inverse[:, None] * target_gain).astype(jnp.bfloat16)
    teacher = jnp.dot(target_in, target_weight.T, preferred_element_type=jnp.float32).astype(jnp.bfloat16)
    entropy = lax.map(row_entropy, logits.reshape(N_DP, TOK, VOCAB)).reshape(TOKENS)
    index = jnp.arange(TOKENS, dtype=jnp.int32)
    local_row = index % TOK
    group = index // TOK
    position = local_row % LEN
    sequence = local_row // LEN
    length = seq_lens[group, sequence]
    valid = jnp.logical_and(position < length - 1, tool_mask == 1).astype(jnp.float32)
    weight_low = (valid * entropy / math.log(VOCAB)).astype(jnp.bfloat16)
    weight = lax.optimization_barrier(weight_low).astype(jnp.float32)
    draft_in = (hidden_float * inverse[:, None] * draft_gain).astype(jnp.bfloat16)
    projection = jnp.dot(draft_in, draft_weight.T, preferred_element_type=jnp.float32)
    error = projection - teacher.astype(jnp.float32)
    scale = 1.0 / math.sqrt(TOKENS)
    grad_out = (weight[:, None] * error * scale).astype(jnp.bfloat16)
    row_loss = 0.5 * weight * lax.optimization_barrier(jnp.sum(error * error, axis=1)) * scale
    grad_weight = jnp.dot(grad_out.T, draft_in, preferred_element_type=jnp.float32)
    grad_normed = jnp.dot(grad_out, draft_weight, preferred_element_type=jnp.float32)
    grad_gain = lax.optimization_barrier(jnp.sum(grad_normed * hidden_float * inverse[:, None], axis=0))
    owner = owners[:, 0]
    member = (owner[:, None] == jnp.arange(N_DP, dtype=jnp.int32)[None, :]).astype(jnp.int32)
    member = member.reshape(N_DP, TOK, N_DP)
    running = jnp.cumsum(member, axis=1)
    rank = (lax.optimization_barrier(jnp.sum(running * member, axis=2)) - 1).reshape(TOKENS)
    target_slot = owner * (N_DP * CAP) + group * CAP + rank
    slot_loss = jnp.zeros((N_DP * N_DP * CAP,), jnp.float32).at[target_slot].set(row_loss)
    return (grad_weight, grad_gain, slot_loss)
```

```python
import math

import jax
import jax.numpy as jnp
from jax import lax
from jax.sharding import Mesh, PartitionSpec as P

VOCAB = 32000
LEN = 128
CAP = 10
EPSILON = 1e-05
DP = ("a", "zh", "zl")
MP = ("x", "b", "c")


def exchange(value, axes):
    return lax.all_to_all(value, axes, split_axis=0, concat_axis=0, tiled=True)


def spread(value, axes):
    copies = lax.axis_size(axes)
    return exchange(jnp.broadcast_to(value[None], (copies,) + value.shape), axes)


def halves(value):
    high = value.astype(jnp.bfloat16)
    low = (value - high.astype(jnp.float32)).astype(jnp.bfloat16)
    return high, low


def softmax_parts(logit_rows):
    values = logit_rows.astype(jnp.float32)
    highest = jnp.max(values, axis=1)
    shifted = values - highest[:, None]
    expsum = jnp.exp(shifted)
    return highest, jnp.sum(expsum, axis=1), jnp.sum(expsum * shifted, axis=1)


def on_device(
    hidden,
    target_gain,
    target_weight,
    draft_gain,
    draft_weight,
    logits,
    seq_lens,
    tool_mask,
    owners,
):
    rows, width = hidden.shape
    features = target_gain.shape[0]
    models = lax.axis_size(MP)
    groups = lax.axis_size(DP)
    pairs = lax.axis_size("zh")
    quads = groups // pairs
    slab = draft_weight.shape[0]
    columns = pairs * slab
    all_rows = quads * rows
    mine = all_rows // models
    a, zl = lax.axis_index("a"), lax.axis_index("zl")
    model = lax.axis_index(MP)
    scale = 1.0 / math.sqrt(rows * groups)

    index = jnp.arange(rows, dtype=jnp.int32)
    length = jnp.where(index < LEN, seq_lens[0, 0], seq_lens[0, 1])
    valid = jnp.logical_and(index % LEN < length - 1, tool_mask == 1)
    owner = owners[:, 0]
    earlier = jnp.logical_and(
        owner[:, None] == owner[None, :], index[:, None] < index[None, :]
    )
    rank = jnp.sum(earlier.astype(jnp.int32), axis=0)
    highest, total, moment = softmax_parts(logits)
    total_high, total_low = halves(total)
    moment_high, moment_low = halves(moment)
    facts = jnp.stack(
        [
            highest.astype(jnp.bfloat16),
            total_high,
            total_low,
            moment_high,
            moment_low,
            valid.astype(jnp.bfloat16),
            owner.astype(jnp.bfloat16),
            rank.astype(jnp.bfloat16),
        ]
    )
    kinds = facts.shape[0]

    with jax.named_scope("wt"):
        wt = lax.dynamic_slice_in_dim(target_weight, zl * slab, slab, axis=0)
        wt = exchange(wt.reshape(slab, models, width).swapaxes(0, 1), MP)
        wt = lax.dynamic_slice_in_dim(wt, a * pairs, pairs, axis=0).reshape(columns, width)
    with jax.named_scope("wd"):
        wd = lax.all_gather(draft_weight, "zh", axis=0, tiled=True)
    with jax.named_scope("rows"):
        carried = jnp.concatenate(
            [hidden, jnp.pad(facts, ((0, 0), (0, width - rows)))], axis=0
        )
        carried = spread(carried, ("a", "zl"))
        features_here = carried[:, :rows].reshape(all_rows, width)
        facts_here = carried[:, rows:, :rows]

    gain_slice = lax.dynamic_slice_in_dim(target_gain, model * width, width)
    wd_float = wd.astype(jnp.float32)
    merged = (wd_float * draft_gain - wt.astype(jnp.float32) * gain_slice).astype(jnp.bfloat16)
    partial = lax.dot_general(
        features_here, merged, (((1,), (1,)), ((), ())), preferred_element_type=jnp.float32
    ).astype(jnp.bfloat16)
    float_rows = features_here.astype(jnp.float32)
    squares = jnp.stack(halves(jnp.sum(float_rows * float_rows, axis=1))).reshape(2, models, mine)
    facts_here = facts_here.swapaxes(0, 1).reshape(kinds, models, mine)
    side = jnp.concatenate([facts_here, squares], axis=0).swapaxes(0, 1)
    side = side.reshape(models, 1, (kinds + 2) * mine)
    lanes = 2 * columns
    side = jnp.pad(side, ((0, 0), (0, 0), (0, 8 * columns - side.shape[2]))).reshape(models, 8, columns)
    with jax.named_scope("sum"):
        got = exchange(
            jnp.concatenate([partial.reshape(models, mine, columns), side], axis=1), MP
        )
    summed = jnp.sum(got[:, :mine].astype(jnp.float32), axis=0)
    side = got[:, mine:].reshape(models, 8 * columns)[:, : (kinds + 2) * mine]
    side = side.reshape(models, kinds + 2, mine).astype(jnp.float32)
    peaks = side[:, 0]
    totals = side[:, 1] + side[:, 2]
    moments = side[:, 3] + side[:, 4]
    peak = jnp.max(peaks, axis=0)
    below = peaks - peak
    factor = jnp.exp(below)
    total = jnp.sum(factor * totals, axis=0)
    moment = jnp.sum(factor * (moments + below * totals), axis=0)
    entropy = jnp.log(total) - moment / total
    weight = (side[0, 5] * entropy / math.log(VOCAB)).astype(jnp.bfloat16).astype(jnp.float32)
    square = jnp.sum(side[:, 8] + side[:, 9], axis=0)
    inverse = lax.rsqrt(square / features + EPSILON)
    error = summed * inverse[:, None]
    loss = 0.5 * weight * jnp.sum(error * error, axis=1) * scale
    slope = (error * (weight * inverse * scale)[:, None]).astype(jnp.bfloat16)
    tail = jnp.concatenate(
        [jnp.stack(halves(loss)), side[0, 6:8].astype(jnp.bfloat16)], axis=0
    )
    tail = jnp.pad(tail, ((0, 4), (0, columns - mine)))
    with jax.named_scope("back"):
        got = spread(jnp.concatenate([slope, tail], axis=0), MP)
    slope = got[:, :mine].reshape(all_rows, columns)
    tail = got[:, mine : mine + 4, :mine].swapaxes(0, 1).reshape(4, all_rows)
    grad = lax.dot_general(
        slope, features_here, (((0,), (0,)), ((), ())), preferred_element_type=jnp.float32
    )
    gain = jnp.sum(grad * wd_float, axis=0)

    named = tail[2][None, :] == jnp.arange(groups, dtype=jnp.bfloat16)[:, None]
    place = jnp.arange(all_rows, dtype=jnp.int32) // rows * CAP + tail[3].astype(jnp.int32)
    there = place[:, None] == jnp.arange(128, dtype=jnp.int32)[None, :]
    zero = jnp.zeros((), jnp.bfloat16)
    named = named.astype(jnp.bfloat16)
    slots = jnp.dot(
        jnp.concatenate([named, named], axis=1),
        jnp.concatenate(
            [jnp.where(there, tail[0][:, None], zero), jnp.where(there, tail[1][:, None], zero)],
            axis=0,
        ),
        preferred_element_type=jnp.float32,
    )
    gain = jnp.broadcast_to(gain.reshape(1, width // 128, 128), (groups, width // 128, 128))
    small = jnp.concatenate(
        [gain, slots[:, None], jnp.zeros((groups, 7 - width // 128, 128), jnp.float32)], axis=1
    )
    with jax.named_scope("small"):
        small = exchange(small, DP)
    with jax.named_scope("grad"):
        parts = exchange(grad.astype(jnp.bfloat16).reshape(pairs, slab, width), "zh")
    grad_weight = jnp.sum(parts.astype(jnp.float32), axis=0) * draft_gain
    grad_gain = jnp.sum(small[:, : width // 128], axis=0).reshape(width)
    slots = small[:, width // 128, : quads * CAP]
    slots = jnp.sum(slots.reshape(2, pairs, 2, quads * CAP), axis=(0, 2))
    slots = slots.reshape(pairs, 2, 2, CAP).transpose(1, 0, 2, 3)
    return (grad_weight, grad_gain, slots.reshape(groups * CAP))


def solution(mesh):
    fine = Mesh(mesh.devices.reshape(2, 8, 2, 4, 2, 2), DP + MP)
    in_specs = (
        P(DP, MP),
        P(),
        P(MP, None),
        P(MP),
        P(DP, MP),
        P(DP, MP),
        P(DP, None),
        P(DP),
        P(DP, None),
    )
    out_specs = (P(DP, MP), P(MP), P(DP))
    return jax.shard_map(
        on_device, mesh=fine, in_specs=in_specs, out_specs=out_specs, check_vma=False
    )
```

```python
import math

import jax
import jax.numpy as jnp
from jax import lax
from jax.sharding import Mesh, PartitionSpec as P


VOCAB = 32000
LEN = 128
CAP = 10
EPSILON = 1e-05
DP = ("a", "zh", "zl")
MP = ("x", "b", "c")


def exchange(value, axes):
    return lax.all_to_all(value, axes, split_axis=0, concat_axis=0, tiled=True)


def spread(value, axes):
    copies = lax.axis_size(axes)
    return exchange(jnp.broadcast_to(value[None], (copies,) + value.shape), axes)


def halves(value):
    high = value.astype(jnp.bfloat16)
    low = (value - high.astype(jnp.float32)).astype(jnp.bfloat16)
    return high, low


def flipped(value, axes):
    sizes = [lax.axis_size(axis) for axis in axes]
    last = math.prod(sizes) - 1
    return lax.ppermute(value, axes, [(k, last - k) for k in range(last + 1)])


def teacher_block(target_weight, a, zl, slab, width):
    x, b, c = (lax.axis_index(axis) for axis in MP)
    quarter = 4 * width

    def piece(column):
        return lax.dynamic_slice(target_weight, (zl * slab, column * quarter), (slab, quarter))

    def turn(swap):
        moves = []
        for k in range(8):
            side, at = divmod(k, 4)
            moves.append((k, at // 2 * 4 + 2 * side + (at % 2) ^ swap))
        return moves

    near = lax.ppermute(piece(2 * a + x % 2), ("a", "x"), turn(0))
    far = lax.ppermute(piece(2 * a + 1 - x % 2), ("a", "x"), turn(1))
    block = jnp.stack([near, far]).reshape(2, slab, 2, 2 * width)

    def halve(block, mine, axis):
        kept = lax.dynamic_index_in_dim(block, mine, axis=block.ndim - 2, keepdims=False)
        sent = lax.dynamic_index_in_dim(block, 1 - mine, axis=block.ndim - 2, keepdims=False)
        return kept, flipped(sent, (axis,))

    kept, came = halve(block, b, "b")
    block = jnp.stack([kept, came], axis=1).reshape(2, 2, slab, 2, width)
    kept, came = halve(block, c, "c")
    block = jnp.stack([kept, came], axis=2)
    block = jnp.where(x % 2 == 1, block[::-1], block)
    block = jnp.where(b == 1, block[:, ::-1], block)
    block = jnp.where(c == 1, block[:, :, ::-1], block)
    return block.reshape(8 * slab, width)


def softmax_parts(logit_rows):
    values = logit_rows.astype(jnp.float32)
    highest = jnp.max(values, axis=1)
    shifted = values - highest[:, None]
    expsum = jnp.exp(shifted)
    return highest, jnp.sum(expsum, axis=1), jnp.sum(expsum * shifted, axis=1)


def on_device(
    hidden,
    target_gain,
    target_weight,
    draft_gain,
    draft_weight,
    logits,
    seq_lens,
    tool_mask,
    owners,
):
    rows, width = hidden.shape
    features = target_gain.shape[0]
    models = lax.axis_size(MP)
    groups = lax.axis_size(DP)
    pairs = lax.axis_size("zh")
    quads = groups // pairs
    slab = draft_weight.shape[0]
    columns = pairs * slab
    all_rows = quads * rows
    mine = all_rows // models
    a, zl = lax.axis_index("a"), lax.axis_index("zl")
    model = lax.axis_index(MP)
    scale = 1.0 / math.sqrt(rows * groups)

    index = jnp.arange(rows, dtype=jnp.int32)
    length = jnp.where(index < LEN, seq_lens[0, 0], seq_lens[0, 1])
    valid = jnp.logical_and(index % LEN < length - 1, tool_mask == 1)
    owner = owners[:, 0]
    earlier = jnp.logical_and(
        owner[:, None] == owner[None, :], index[:, None] < index[None, :]
    )
    rank = jnp.sum(earlier.astype(jnp.int32), axis=0)
    highest, total, moment = softmax_parts(logits)
    total_high, total_low = halves(total)
    moment_high, moment_low = halves(moment)
    facts = jnp.stack(
        [
            highest.astype(jnp.bfloat16),
            total_high,
            total_low,
            moment_high,
            moment_low,
            valid.astype(jnp.bfloat16),
            owner.astype(jnp.bfloat16),
            rank.astype(jnp.bfloat16),
        ]
    )
    kinds = facts.shape[0]

    wd = spread(draft_weight, "zh").reshape(columns, width)
    carried = jnp.concatenate(
        [hidden, jnp.pad(facts, ((0, 0), (0, width - rows)))], axis=0
    )
    carried = jnp.stack(
        [carried] + [flipped(carried, axes) for axes in (("zl",), ("a",), ("a", "zl"))]
    )
    features_here = carried[:, :rows].reshape(all_rows, width)
    facts_here = carried[:, rows:, :rows]
    wt = teacher_block(target_weight, a, zl, slab, width)

    gain_slice = lax.dynamic_slice_in_dim(target_gain, model * width, width)
    wd_float = wd.astype(jnp.float32)
    merged = (wd_float * draft_gain - wt.astype(jnp.float32) * gain_slice).astype(jnp.bfloat16)
    partial = lax.dot_general(
        features_here, merged, (((1,), (1,)), ((), ())), preferred_element_type=jnp.float32
    ).astype(jnp.bfloat16)
    float_rows = features_here.astype(jnp.float32)
    squares = jnp.stack(halves(jnp.sum(float_rows * float_rows, axis=1))).reshape(2, models, mine)
    facts_here = facts_here.swapaxes(0, 1).reshape(kinds, models, mine)
    side = jnp.concatenate([facts_here, squares], axis=0).swapaxes(0, 1)
    side = side.reshape(models, 1, (kinds + 2) * mine)
    side = jnp.pad(side, ((0, 0), (0, 0), (0, 8 * columns - side.shape[2]))).reshape(models, 8, columns)
    got = exchange(
        jnp.concatenate([partial.reshape(models, mine, columns), side], axis=1), MP
    )
    summed = jnp.sum(got[:, :mine].astype(jnp.float32), axis=0)
    side = got[:, mine:].reshape(models, 8 * columns)[:, : (kinds + 2) * mine]
    side = side.reshape(models, kinds + 2, mine).astype(jnp.float32)
    peaks = side[:, 0]
    totals = side[:, 1] + side[:, 2]
    moments = side[:, 3] + side[:, 4]
    peak = jnp.max(peaks, axis=0)
    below = peaks - peak
    factor = jnp.exp(below)
    total = jnp.sum(factor * totals, axis=0)
    moment = jnp.sum(factor * (moments + below * totals), axis=0)
    entropy = jnp.log(total) - moment / total
    weight = (side[0, 5] * entropy / math.log(VOCAB)).astype(jnp.bfloat16).astype(jnp.float32)
    square = jnp.sum(side[:, 8] + side[:, 9], axis=0)
    inverse = lax.rsqrt(square / features + EPSILON)
    error = summed * inverse[:, None]
    loss = 0.5 * weight * jnp.sum(error * error, axis=1) * scale
    slope = (error * (weight * inverse * scale)[:, None]).astype(jnp.bfloat16)
    tail = jnp.concatenate(
        [jnp.stack(halves(loss)), side[0, 6:8].astype(jnp.bfloat16)], axis=0
    )
    tail = jnp.pad(tail, ((0, 4), (0, columns - mine)))
    got = spread(jnp.concatenate([slope, tail], axis=0), MP)
    slope = got[:, :mine].reshape(all_rows, columns)
    tail = got[:, mine : mine + 4, :mine].swapaxes(0, 1).reshape(4, all_rows)
    grad = lax.dot_general(
        slope, features_here, (((0,), (0,)), ((), ())), preferred_element_type=jnp.float32
    )
    gain = jnp.sum(grad * wd_float, axis=0)

    named = tail[2][None, :] == jnp.arange(groups, dtype=jnp.bfloat16)[:, None]
    quad = (jnp.arange(all_rows, dtype=jnp.int32) // rows) ^ (2 * a + zl)
    place = quad * CAP + tail[3].astype(jnp.int32)
    there = place[:, None] == jnp.arange(128, dtype=jnp.int32)[None, :]
    zero = jnp.zeros((), jnp.bfloat16)
    named = named.astype(jnp.bfloat16)
    slots = jnp.dot(
        jnp.concatenate([named, named], axis=1),
        jnp.concatenate(
            [jnp.where(there, tail[0][:, None], zero), jnp.where(there, tail[1][:, None], zero)],
            axis=0,
        ),
        preferred_element_type=jnp.float32,
    )
    parts = exchange(grad.astype(jnp.bfloat16).reshape(pairs, slab, width), "zh")
    small = jnp.concatenate([slots, gain.reshape(width // 128, 128), jnp.zeros((4, 128), jnp.float32)])
    small = lax.all_gather(small, DP)
    grad_weight = jnp.sum(parts.astype(jnp.float32), axis=0) * draft_gain
    grad_gain = jnp.sum(small[:, groups : groups + width // 128], axis=0).reshape(width)
    slots = lax.dynamic_index_in_dim(small, lax.axis_index(DP), axis=1, keepdims=False)[:, : quads * CAP]
    slots = jnp.sum(slots.reshape(2, pairs, 2, quads * CAP), axis=(0, 2))
    slots = slots.reshape(pairs, 2, 2, CAP).transpose(1, 0, 2, 3)
    return (grad_weight, grad_gain, slots.reshape(groups * CAP))


def solution(mesh):
    fine = Mesh(mesh.devices.reshape(2, 8, 2, 4, 2, 2), DP + MP)
    in_specs = (
        P(DP, MP),
        P(),
        P(MP, None),
        P(MP),
        P(DP, MP),
        P(DP, MP),
        P(DP, None),
        P(DP),
        P(DP, None),
    )
    out_specs = (P(DP, MP), P(MP), P(DP))

    return jax.shard_map(
        on_device, mesh=fine, in_specs=in_specs, out_specs=out_specs, check_vma=False
    )
```

```python
import math

import jax
import jax.numpy as jnp
from jax import lax
from jax.experimental import pallas as pl
from jax.experimental.pallas import tpu as pltpu
from jax.sharding import Mesh, PartitionSpec as P


VOCAB = 32000
LEN = 128
CAP = 10
EPSILON = 1e-05
DP = ("a", "zh", "zl")
MP = ("x", "b", "c")


def exchange(value, axes):
    return lax.all_to_all(value, axes, split_axis=0, concat_axis=0, tiled=True)


def spread(value, axes):
    copies = lax.axis_size(axes)
    return exchange(jnp.broadcast_to(value[None], (copies,) + value.shape), axes)


def halves(value):
    high = value.astype(jnp.bfloat16)
    low = (value - high.astype(jnp.float32)).astype(jnp.bfloat16)
    return high, low


def flipped(value, axes):
    sizes = [lax.axis_size(axis) for axis in axes]
    last = math.prod(sizes) - 1
    return lax.ppermute(value, axes, [(k, last - k) for k in range(last + 1)])


def teacher_block(target_weight, a, zl, slab, width):
    x, b, c = (lax.axis_index(axis) for axis in MP)
    quarter = 4 * width

    def piece(column):
        return lax.dynamic_slice(target_weight, (zl * slab, column * quarter), (slab, quarter))

    def turn(swap):
        moves = []
        for k in range(8):
            side, at = divmod(k, 4)
            moves.append((k, at // 2 * 4 + 2 * side + (at % 2) ^ swap))
        return moves

    near = lax.ppermute(piece(2 * a + x % 2), ("a", "x"), turn(0))
    far = lax.ppermute(piece(2 * a + 1 - x % 2), ("a", "x"), turn(1))

    def halve(parts, mine, axis):
        half = parts[0].shape[1] // 2

        def side(which):
            return jnp.concatenate(
                [lax.dynamic_slice_in_dim(part, which * half, half, axis=1) for part in parts]
            )

        return side(mine), flipped(side(1 - mine), (axis,))

    parts = halve((near, far), b, "b")
    parts = halve(parts, c, "c")
    return [part.reshape(4, slab, width) for part in parts], 4 * (x % 2) + 2 * b + c


def project(place, own, left, right, cross, wd, kept, came, gains, side, out):
    slab = wd.shape[1]
    mine = out.shape[1] - side.shape[1]
    rows = 4 * mine
    here = place[0]
    draft_gain, target_gain = gains[0:1], gains[1:2]
    for pair in range(4):
        merged = []
        for k in (2 * pair, 2 * pair + 1):
            away = here ^ k
            at = away // 2 % 2 * 2 + away // 4
            parts = kept[at], came[at]
            wt = jnp.where(away % 2 == 1, parts[1].astype(jnp.float32), parts[0].astype(jnp.float32))
            merged.append(wd[k].astype(jnp.float32) * draft_gain - wt * target_gain)
        merged = jnp.concatenate(merged).astype(jnp.bfloat16)
        lanes = slice(pair * 2 * slab, (pair + 1) * 2 * slab)
        for quad, block in enumerate((own, left, right, cross)):
            value = lax.dot_general(
                block[:rows], merged, (((1,), (1,)), ((), ())), preferred_element_type=jnp.float32
            )
            out[4 * quad : 4 * quad + 4, :mine, lanes] = value.astype(jnp.bfloat16).reshape(
                4, mine, 2 * slab
            )
    out[:, mine:] = side[...]


def softmax_parts(logit_rows):
    values = logit_rows.astype(jnp.float32)
    highest = jnp.max(values, axis=1)
    shifted = values - highest[:, None]
    expsum = jnp.exp(shifted)
    return highest, jnp.sum(expsum, axis=1), jnp.sum(expsum * shifted, axis=1)


def on_device(
    hidden,
    target_gain,
    target_weight,
    draft_gain,
    draft_weight,
    logits,
    seq_lens,
    tool_mask,
    owners,
):
    rows, width = hidden.shape
    features = target_gain.shape[0]
    models = lax.axis_size(MP)
    groups = lax.axis_size(DP)
    pairs = lax.axis_size("zh")
    quads = groups // pairs
    slab = draft_weight.shape[0]
    columns = pairs * slab
    all_rows = quads * rows
    mine = all_rows // models
    a, zl = lax.axis_index("a"), lax.axis_index("zl")
    model = lax.axis_index(MP)
    scale = 1.0 / math.sqrt(rows * groups)

    index = jnp.arange(rows, dtype=jnp.int32)
    length = jnp.where(index < LEN, seq_lens[0, 0], seq_lens[0, 1])
    valid = jnp.logical_and(index % LEN < length - 1, tool_mask == 1)
    owner = owners[:, 0]
    earlier = jnp.logical_and(
        owner[:, None] == owner[None, :], index[:, None] < index[None, :]
    )
    rank = jnp.sum(earlier.astype(jnp.int32), axis=0)
    highest, total, moment = softmax_parts(logits)
    total_high, total_low = halves(total)
    moment_high, moment_low = halves(moment)
    facts = jnp.stack(
        [
            highest.astype(jnp.bfloat16),
            total_high,
            total_low,
            moment_high,
            moment_low,
            valid.astype(jnp.bfloat16),
            owner.astype(jnp.bfloat16),
            rank.astype(jnp.bfloat16),
        ]
    )
    kinds = facts.shape[0]

    wd = spread(draft_weight, "zh").reshape(columns, width)
    carried = jnp.concatenate(
        [hidden, jnp.pad(facts, ((0, 0), (0, width - rows)))], axis=0
    )
    blocks = [carried]
    blocks += [flipped(carried, axes) for axes in (("zl",), ("a",), ("a", "zl"))]
    carried = jnp.stack(blocks)
    features_here = carried[:, :rows].reshape(all_rows, width)
    facts_here = carried[:, rows:, :rows]
    (kept, came), place = teacher_block(target_weight, a, zl, slab, width)

    gain_slice = lax.dynamic_slice_in_dim(target_gain, model * width, width)
    gains = jnp.stack([draft_gain, gain_slice])
    float_rows = features_here.astype(jnp.float32)
    squares = jnp.stack(halves(jnp.sum(float_rows * float_rows, axis=1))).reshape(2, models, mine)
    facts_here = facts_here.swapaxes(0, 1).reshape(kinds, models, mine)
    side = jnp.concatenate([facts_here, squares], axis=0).swapaxes(0, 1)
    side = side.reshape(models, 1, (kinds + 2) * mine)
    side = jnp.pad(side, ((0, 0), (0, 0), (0, 8 * columns - side.shape[2]))).reshape(models, 8, columns)
    partial = pl.pallas_call(
        project,
        out_shape=jax.ShapeDtypeStruct((models, mine + 8, columns), jnp.bfloat16),
        in_specs=[pl.BlockSpec(memory_space=pltpu.SMEM)]
        + [pl.BlockSpec(memory_space=pltpu.VMEM)] * 9,
        out_specs=pl.BlockSpec(memory_space=pltpu.VMEM),
        cost_estimate=pl.CostEstimate(
            flops=2 * all_rows * width * columns,
            bytes_accessed=2 * (2 * all_rows * width + 2 * columns * width),
            transcendentals=0,
        ),
        compiler_params=pltpu.CompilerParams(vmem_limit_bytes=16 * 2**20),
        name="project",
    )(place.reshape(1), *blocks, wd.reshape(pairs, slab, width), kept, came, gains, side)
    got = exchange(partial, MP)
    summed = jnp.sum(got[:, :mine].astype(jnp.float32), axis=0)
    side = got[:, mine:].reshape(models, 8 * columns)[:, : (kinds + 2) * mine]
    side = side.reshape(models, kinds + 2, mine).astype(jnp.float32)
    peaks = side[:, 0]
    totals = side[:, 1] + side[:, 2]
    moments = side[:, 3] + side[:, 4]
    peak = jnp.max(peaks, axis=0)
    below = peaks - peak
    factor = jnp.exp(below)
    total = jnp.sum(factor * totals, axis=0)
    moment = jnp.sum(factor * (moments + below * totals), axis=0)
    entropy = jnp.log(total) - moment / total
    weight = (side[0, 5] * entropy / math.log(VOCAB)).astype(jnp.bfloat16).astype(jnp.float32)
    square = jnp.sum(side[:, 8] + side[:, 9], axis=0)
    inverse = lax.rsqrt(square / features + EPSILON)
    error = summed * inverse[:, None]
    loss = 0.5 * weight * jnp.sum(error * error, axis=1) * scale
    slope = (error * (weight * inverse * scale)[:, None]).astype(jnp.bfloat16)
    tail = jnp.concatenate(
        [jnp.stack(halves(loss)), side[0, 6:8].astype(jnp.bfloat16)], axis=0
    )
    tail = jnp.pad(tail, ((0, 4), (0, columns - mine)))
    got = spread(jnp.concatenate([slope, tail], axis=0), MP)
    slope = got[:, :mine].reshape(all_rows, columns)
    tail = got[:, mine : mine + 4, :mine].swapaxes(0, 1).reshape(4, all_rows)
    grad = lax.dot_general(
        slope, features_here, (((0,), (0,)), ((), ())), preferred_element_type=jnp.float32
    )
    gain = jnp.sum(grad * wd.astype(jnp.float32), axis=0)

    named = tail[2][None, :] == jnp.arange(groups, dtype=jnp.bfloat16)[:, None]
    quad = (jnp.arange(all_rows, dtype=jnp.int32) // rows) ^ (2 * a + zl)
    place = quad * CAP + tail[3].astype(jnp.int32)
    there = place[:, None] == jnp.arange(128, dtype=jnp.int32)[None, :]
    zero = jnp.zeros((), jnp.bfloat16)
    named = named.astype(jnp.bfloat16)
    slots = jnp.dot(
        jnp.concatenate([named, named], axis=1),
        jnp.concatenate(
            [jnp.where(there, tail[0][:, None], zero), jnp.where(there, tail[1][:, None], zero)],
            axis=0,
        ),
        preferred_element_type=jnp.float32,
    )
    parts = exchange(grad.astype(jnp.bfloat16).reshape(pairs, slab, width), "zh")
    slots = slots.reshape(2, pairs, 2, 128)

    def toward(swap_a, swap_zl):
        for_them = lax.dynamic_index_in_dim(slots, a ^ swap_a, axis=0, keepdims=False)
        for_them = lax.dynamic_index_in_dim(for_them, zl ^ swap_zl, axis=1, keepdims=False)
        return jnp.concatenate([for_them, gain.reshape(width // 128, 128)], axis=0)

    small = toward(0, 0)
    small += flipped(toward(0, 1), ("zl",))
    small += flipped(toward(1, 0), ("a",))
    small += flipped(toward(1, 1), ("a", "zl"))
    zh = lax.axis_index("zh")
    source = jnp.arange(pairs, dtype=jnp.int32)[:, None, None]
    slots = jnp.where(source == zh, small[None, :pairs], 0.0).reshape(pairs * pairs, 128)
    small = jnp.concatenate([slots, small[pairs:], jnp.zeros((4, 128), jnp.float32)], axis=0)
    for step in (1, 2, 4):
        moves = [(k, k ^ step) for k in range(pairs)]
        small += lax.ppermute(small, "zh", moves)
    grad_weight = jnp.sum(parts.astype(jnp.float32), axis=0) * draft_gain
    grad_gain = small[pairs * pairs : pairs * pairs + width // 128].reshape(width)
    slots = lax.dynamic_index_in_dim(
        small[: pairs * pairs].reshape(pairs, pairs, 128), zh, axis=1, keepdims=False
    )[:, : quads * CAP]
    slots = slots.reshape(pairs, 2, 2, CAP).transpose(1, 0, 2, 3)
    return (grad_weight, grad_gain, slots.reshape(groups * CAP))


def solution(mesh):
    fine = Mesh(mesh.devices.reshape(2, 8, 2, 4, 2, 2), DP + MP)
    in_specs = (
        P(DP, MP),
        P(),
        P(MP, None),
        P(MP),
        P(DP, MP),
        P(DP, MP),
        P(DP, None),
        P(DP),
        P(DP, None),
    )
    out_specs = (P(DP, MP), P(MP), P(DP))

    return jax.shard_map(
        on_device, mesh=fine, in_specs=in_specs, out_specs=out_specs, check_vma=False
    )
```

```python
import math

import jax
import jax.numpy as jnp
from jax import lax
from jax.experimental import pallas as pl
from jax.experimental.pallas import tpu as pltpu
from jax.sharding import Mesh, PartitionSpec as P


VOCAB = 32000
LEN = 128
CAP = 10
EPSILON = 1e-05
DP = ("a", "zh", "zl")
MP = ("x", "b", "c")


def exchange(value, axes):
    return lax.all_to_all(value, axes, split_axis=0, concat_axis=0, tiled=True)


def spread(value, axes):
    copies = lax.axis_size(axes)
    return exchange(jnp.broadcast_to(value[None], (copies,) + value.shape), axes)


def halves(value):
    high = value.astype(jnp.bfloat16)
    low = (value - high.astype(jnp.float32)).astype(jnp.bfloat16)
    return high, low


def flipped(value, axes):
    sizes = [lax.axis_size(axis) for axis in axes]
    last = math.prod(sizes) - 1
    return lax.ppermute(value, axes, [(k, last - k) for k in range(last + 1)])


def teacher_block(target_weight, a, zl, slab, width):
    x, b, c = (lax.axis_index(axis) for axis in MP)
    quarter = 4 * width

    def piece(column):
        return lax.dynamic_slice(target_weight, (zl * slab, column * quarter), (slab, quarter))

    def turn(swap):
        moves = []
        for k in range(8):
            side, at = divmod(k, 4)
            moves.append((k, at // 2 * 4 + 2 * side + (at % 2) ^ swap))
        return moves

    near = lax.ppermute(piece(2 * a + x % 2), ("a", "x"), turn(0))
    far = lax.ppermute(piece(2 * a + 1 - x % 2), ("a", "x"), turn(1))

    def halve(parts, mine, axis):
        half = parts[0].shape[1] // 2

        def side(which):
            return jnp.concatenate(
                [lax.dynamic_slice_in_dim(part, which * half, half, axis=1) for part in parts]
            )

        return side(mine), flipped(side(1 - mine), (axis,))

    parts = halve((near, far), b, "b")
    parts = halve(parts, c, "c")
    return [part.reshape(4, slab, width) for part in parts], 4 * (x % 2) + 2 * b + c


def project(place, near, far, wd, kept, came, gains, side, out):
    slab = wd.shape[1]
    mine = out.shape[1] - side.shape[1]
    here = place[0]
    draft_gain, target_gain = gains[0:1], gains[1:2]
    for pair in range(4):
        merged = []
        for k in (2 * pair, 2 * pair + 1):
            away = here ^ k
            at = away // 2 % 2 * 2 + away // 4
            parts = kept[at], came[at]
            wt = jnp.where(away % 2 == 1, parts[1].astype(jnp.float32), parts[0].astype(jnp.float32))
            merged.append(wd[k].astype(jnp.float32) * draft_gain - wt * target_gain)
        merged = jnp.concatenate(merged).astype(jnp.bfloat16)
        lanes = slice(pair * 2 * slab, (pair + 1) * 2 * slab)
        for half, block in enumerate((near, far)):
            value = lax.dot_general(
                block[...], merged, (((1,), (1,)), ((), ())), preferred_element_type=jnp.float32
            )
            out[8 * half : 8 * half + 8, :mine, lanes] = value.astype(jnp.bfloat16).reshape(
                8, mine, 2 * slab
            )
    out[:, mine:] = side[...]


def softmax_parts(logit_rows):
    values = logit_rows.astype(jnp.float32)
    highest = jnp.max(values, axis=1)
    shifted = values - highest[:, None]
    expsum = jnp.exp(shifted)
    return highest, jnp.sum(expsum, axis=1), jnp.sum(expsum * shifted, axis=1)


def on_device(
    hidden,
    target_gain,
    target_weight,
    draft_gain,
    draft_weight,
    logits,
    seq_lens,
    tool_mask,
    owners,
):
    rows, width = hidden.shape
    features = target_gain.shape[0]
    models = lax.axis_size(MP)
    groups = lax.axis_size(DP)
    pairs = lax.axis_size("zh")
    quads = groups // pairs
    slab = draft_weight.shape[0]
    columns = pairs * slab
    all_rows = quads * rows
    mine = all_rows // models
    a, zl = lax.axis_index("a"), lax.axis_index("zl")
    model = lax.axis_index(MP)
    scale = 1.0 / math.sqrt(rows * groups)

    index = jnp.arange(rows, dtype=jnp.int32)
    length = jnp.where(index < LEN, seq_lens[0, 0], seq_lens[0, 1])
    valid = jnp.logical_and(index % LEN < length - 1, tool_mask == 1)
    owner = owners[:, 0]
    earlier = jnp.logical_and(
        owner[:, None] == owner[None, :], index[:, None] < index[None, :]
    )
    rank = jnp.sum(earlier.astype(jnp.int32), axis=0)
    highest, total, moment = softmax_parts(logits)
    total_high, total_low = halves(total)
    moment_high, moment_low = halves(moment)
    facts = jnp.stack(
        [
            highest.astype(jnp.bfloat16),
            total_high,
            total_low,
            moment_high,
            moment_low,
            valid.astype(jnp.bfloat16),
            owner.astype(jnp.bfloat16),
            rank.astype(jnp.bfloat16),
        ]
    )
    kinds = facts.shape[0]

    wd = spread(draft_weight, "zh").reshape(columns, width)
    near = jnp.concatenate([hidden, flipped(hidden, ("a",))], axis=0)
    far = flipped(near, ("zl",))
    facts_here = jnp.stack([facts, flipped(facts, ("a",))])
    facts_here = jnp.concatenate([facts_here, flipped(facts_here, ("zl",))], axis=0)
    features_here = jnp.concatenate([near, far], axis=0)
    (kept, came), place = teacher_block(target_weight, a, zl, slab, width)

    gain_slice = lax.dynamic_slice_in_dim(target_gain, model * width, width)
    gains = jnp.stack([draft_gain, gain_slice])
    float_rows = features_here.astype(jnp.float32)
    squares = jnp.stack(halves(jnp.sum(float_rows * float_rows, axis=1))).reshape(2, models, mine)
    facts_here = facts_here.swapaxes(0, 1).reshape(kinds, models, mine)
    side = jnp.concatenate([facts_here, squares], axis=0).swapaxes(0, 1)
    side = side.reshape(models, 1, (kinds + 2) * mine)
    side = jnp.pad(side, ((0, 0), (0, 0), (0, 8 * columns - side.shape[2]))).reshape(models, 8, columns)
    partial = pl.pallas_call(
        project,
        out_shape=jax.ShapeDtypeStruct((models, mine + 8, columns), jnp.bfloat16),
        in_specs=[pl.BlockSpec(memory_space=pltpu.SMEM)]
        + [pl.BlockSpec(memory_space=pltpu.VMEM)] * 7,
        out_specs=pl.BlockSpec(memory_space=pltpu.VMEM),
        cost_estimate=pl.CostEstimate(
            flops=2 * all_rows * width * columns,
            bytes_accessed=2 * (2 * all_rows * width + 2 * columns * width),
            transcendentals=0,
        ),
        compiler_params=pltpu.CompilerParams(vmem_limit_bytes=16 * 2**20),
        name="project",
    )(place.reshape(1), near, far, wd.reshape(pairs, slab, width), kept, came, gains, side)
    got = exchange(partial, MP)
    summed = jnp.sum(got[:, :mine].astype(jnp.float32), axis=0)
    side = got[:, mine:].reshape(models, 8 * columns)[:, : (kinds + 2) * mine]
    side = side.reshape(models, kinds + 2, mine).astype(jnp.float32)
    peaks = side[:, 0]
    totals = side[:, 1] + side[:, 2]
    moments = side[:, 3] + side[:, 4]
    peak = jnp.max(peaks, axis=0)
    below = peaks - peak
    factor = jnp.exp(below)
    total = jnp.sum(factor * totals, axis=0)
    moment = jnp.sum(factor * (moments + below * totals), axis=0)
    entropy = jnp.log(total) - moment / total
    weight = (side[0, 5] * entropy / math.log(VOCAB)).astype(jnp.bfloat16).astype(jnp.float32)
    square = jnp.sum(side[:, 8] + side[:, 9], axis=0)
    inverse = lax.rsqrt(square / features + EPSILON)
    error = summed * inverse[:, None]
    loss = 0.5 * weight * jnp.sum(error * error, axis=1) * scale
    slope = (error * (weight * inverse * scale)[:, None]).astype(jnp.bfloat16)
    tail = jnp.concatenate(
        [jnp.stack(halves(loss)), side[0, 6:8].astype(jnp.bfloat16)], axis=0
    )
    tail = jnp.pad(tail, ((0, 4), (0, columns - mine)))
    got = spread(jnp.concatenate([slope, tail], axis=0), MP)
    slope = got[:, :mine].reshape(all_rows, columns)
    tail = got[:, mine : mine + 4, :mine].swapaxes(0, 1).reshape(4, all_rows)
    grad = lax.dot_general(
        slope, features_here, (((0,), (0,)), ((), ())), preferred_element_type=jnp.float32
    )
    gain = jnp.sum(grad * wd.astype(jnp.float32), axis=0)

    named = tail[2][None, :] == jnp.arange(groups, dtype=jnp.bfloat16)[:, None]
    block = jnp.arange(all_rows, dtype=jnp.int32) // rows
    quad = 2 * (a ^ (block % 2)) + (zl ^ (block // 2))
    place = quad * CAP + tail[3].astype(jnp.int32)
    there = place[:, None] == jnp.arange(128, dtype=jnp.int32)[None, :]
    zero = jnp.zeros((), jnp.bfloat16)
    named = named.astype(jnp.bfloat16)
    slots = jnp.dot(
        jnp.concatenate([named, named], axis=1),
        jnp.concatenate(
            [jnp.where(there, tail[0][:, None], zero), jnp.where(there, tail[1][:, None], zero)],
            axis=0,
        ),
        preferred_element_type=jnp.float32,
    )
    slots = slots.reshape(2, pairs, 2, 128)

    def toward(swap_a, swap_zl):
        for_them = lax.dynamic_index_in_dim(slots, a ^ swap_a, axis=0, keepdims=False)
        for_them = lax.dynamic_index_in_dim(for_them, zl ^ swap_zl, axis=1, keepdims=False)
        return jnp.concatenate([for_them, gain.reshape(width // 128, 128)], axis=0)

    small = toward(0, 0)
    small += flipped(toward(0, 1), ("zl",))
    small += flipped(toward(1, 0), ("a",))
    small += flipped(toward(1, 1), ("a", "zl"))
    gain_halves = [half.reshape(1, width) for half in halves(small[pairs:])]
    extra = jnp.broadcast_to(jnp.concatenate(gain_halves)[None], (pairs, 2, width))
    slot_halves = jnp.concatenate(halves(small[:pairs]), axis=1)[:, None]
    extra = jnp.concatenate([extra, jnp.pad(slot_halves, ((0, 0), (0, 0), (0, width - 256)))], axis=1)
    extra = jnp.pad(extra, ((0, 0), (0, 5), (0, 0)))
    parts = exchange(
        jnp.concatenate([grad.astype(jnp.bfloat16).reshape(pairs, slab, width), extra], axis=1),
        "zh",
    )
    grad_weight = jnp.sum(parts[:, :slab].astype(jnp.float32), axis=0) * draft_gain
    extra = parts[:, slab : slab + 3].astype(jnp.float32)
    grad_gain = jnp.sum(extra[:, :2], axis=(0, 1))
    slots = extra[:, 2, : quads * CAP] + extra[:, 2, 128 : 128 + quads * CAP]
    slots = slots.reshape(pairs, 2, 2, CAP).transpose(1, 0, 2, 3)
    return (grad_weight, grad_gain, slots.reshape(groups * CAP))


def solution(mesh):
    fine = Mesh(mesh.devices.reshape(2, 8, 2, 4, 2, 2), DP + MP)
    in_specs = (
        P(DP, MP),
        P(),
        P(MP, None),
        P(MP),
        P(DP, MP),
        P(DP, MP),
        P(DP, None),
        P(DP),
        P(DP, None),
    )
    out_specs = (P(DP, MP), P(MP), P(DP))

    return jax.shard_map(
        on_device, mesh=fine, in_specs=in_specs, out_specs=out_specs, check_vma=False
    )
```

```python
import math

import jax
import jax.numpy as jnp
from jax import lax
from jax.experimental import pallas as pl
from jax.experimental.pallas import tpu as pltpu
from jax.sharding import Mesh, PartitionSpec as P


VOCAB = 32000
LEN = 128
CAP = 10
EPSILON = 1e-05
DP = ("a", "zh", "zl")
MP = ("x", "b", "c")


def exchange(value, axes):
    return lax.all_to_all(value, axes, split_axis=0, concat_axis=0, tiled=True)


def spread(value, axes):
    copies = lax.axis_size(axes)
    return exchange(jnp.broadcast_to(value[None], (copies,) + value.shape), axes)


def halves(value):
    high = value.astype(jnp.bfloat16)
    low = (value - high.astype(jnp.float32)).astype(jnp.bfloat16)
    return high, low


def flipped(value, axes):
    sizes = [lax.axis_size(axis) for axis in axes]
    last = math.prod(sizes) - 1
    return lax.ppermute(value, axes, [(k, last - k) for k in range(last + 1)])


def teacher_block(target_weight, a, zl, slab, width):
    x, b, c = (lax.axis_index(axis) for axis in MP)
    quarter = 4 * width

    def piece(column):
        return lax.dynamic_slice(target_weight, (zl * slab, column * quarter), (slab, quarter))

    def turn(swap):
        moves = []
        for k in range(8):
            side, at = divmod(k, 4)
            moves.append((k, at // 2 * 4 + 2 * side + (at % 2) ^ swap))
        return moves

    near = lax.ppermute(piece(2 * a + x % 2), ("a", "x"), turn(0))
    far = lax.ppermute(piece(2 * a + 1 - x % 2), ("a", "x"), turn(1))

    def halve(parts, mine, axis):
        half = parts[0].shape[1] // 2

        def side(which):
            return jnp.concatenate(
                [lax.dynamic_slice_in_dim(part, which * half, half, axis=1) for part in parts]
            )

        return side(mine), flipped(side(1 - mine), (axis,))

    parts = halve((near, far), b, "b")
    parts = halve(parts, c, "c")
    return [part.reshape(4, slab, width) for part in parts], 4 * (x % 2) + 2 * b + c


def project(place, own, across, beside, both, wd, kept, came, gains, side, out):
    slab = wd.shape[1]
    mine = out.shape[1] - side.shape[1]
    here = place[0]
    draft_gain, target_gain = gains[0:1], gains[1:2]
    for pair in range(4):
        merged = []
        for k in (2 * pair, 2 * pair + 1):
            away = here ^ k
            at = away // 2 % 2 * 2 + away // 4
            parts = kept[at], came[at]
            wt = jnp.where(away % 2 == 1, parts[1].astype(jnp.float32), parts[0].astype(jnp.float32))
            merged.append(wd[k].astype(jnp.float32) * draft_gain - wt * target_gain)
        merged = jnp.concatenate(merged).astype(jnp.bfloat16)
        lanes = slice(pair * 2 * slab, (pair + 1) * 2 * slab)
        for quad, block in enumerate((own, across, beside, both)):
            value = lax.dot_general(
                block[: 4 * mine],
                merged,
                (((1,), (1,)), ((), ())),
                preferred_element_type=jnp.float32,
            )
            out[4 * quad : 4 * quad + 4, :mine, lanes] = value.astype(jnp.bfloat16).reshape(
                4, mine, 2 * slab
            )
    out[:, mine:] = side[...]


def softmax_parts(logit_rows):
    values = logit_rows.astype(jnp.float32)
    highest = jnp.max(values, axis=1)
    shifted = values - highest[:, None]
    expsum = jnp.exp(shifted)
    return highest, jnp.sum(expsum, axis=1), jnp.sum(expsum * shifted, axis=1)


def on_device(
    hidden,
    target_gain,
    target_weight,
    draft_gain,
    draft_weight,
    logits,
    seq_lens,
    tool_mask,
    owners,
):
    rows, width = hidden.shape
    features = target_gain.shape[0]
    models = lax.axis_size(MP)
    groups = lax.axis_size(DP)
    pairs = lax.axis_size("zh")
    quads = groups // pairs
    slab = draft_weight.shape[0]
    columns = pairs * slab
    all_rows = quads * rows
    mine = all_rows // models
    a, zl = lax.axis_index("a"), lax.axis_index("zl")
    model = lax.axis_index(MP)
    scale = 1.0 / math.sqrt(rows * groups)

    index = jnp.arange(rows, dtype=jnp.int32)
    length = jnp.where(index < LEN, seq_lens[0, 0], seq_lens[0, 1])
    valid = jnp.logical_and(index % LEN < length - 1, tool_mask == 1)
    owner = owners[:, 0]
    earlier = jnp.logical_and(
        owner[:, None] == owner[None, :], index[:, None] < index[None, :]
    )
    rank = jnp.sum(earlier.astype(jnp.int32), axis=0)
    highest, total, moment = softmax_parts(logits)
    total_high, total_low = halves(total)
    moment_high, moment_low = halves(moment)
    facts = jnp.stack(
        [
            highest.astype(jnp.bfloat16),
            total_high,
            total_low,
            moment_high,
            moment_low,
            valid.astype(jnp.bfloat16),
            owner.astype(jnp.bfloat16),
            rank.astype(jnp.bfloat16),
        ]
    )
    kinds = facts.shape[0]

    wd = spread(draft_weight, "zh").reshape(columns, width)
    own = jnp.concatenate([hidden, jnp.pad(facts, ((0, 0), (0, width - rows)))], axis=0)
    across = flipped(own, ("a",))
    beside = flipped(own, ("zl",))
    both = flipped(across, ("zl",))
    blocks = (own, across, beside, both)
    facts_here = jnp.stack([block[rows:, :rows] for block in blocks])
    (kept, came), place = teacher_block(target_weight, a, zl, slab, width)

    gain_slice = lax.dynamic_slice_in_dim(target_gain, model * width, width)
    gains = jnp.stack([draft_gain, gain_slice])
    squares = [jnp.sum(block[:rows].astype(jnp.float32) ** 2, axis=1) for block in blocks]
    squares = jnp.stack(halves(jnp.stack(squares))).reshape(2, models, mine)
    facts_here = facts_here.swapaxes(0, 1).reshape(kinds, models, mine)
    side = jnp.concatenate([facts_here, squares], axis=0).swapaxes(0, 1)
    side = side.reshape(models, 1, (kinds + 2) * mine)
    side = jnp.pad(side, ((0, 0), (0, 0), (0, 8 * columns - side.shape[2]))).reshape(models, 8, columns)
    partial = pl.pallas_call(
        project,
        out_shape=jax.ShapeDtypeStruct((models, mine + 8, columns), jnp.bfloat16),
        in_specs=[pl.BlockSpec(memory_space=pltpu.SMEM)]
        + [pl.BlockSpec(memory_space=pltpu.VMEM)] * 9,
        out_specs=pl.BlockSpec(memory_space=pltpu.VMEM),
        cost_estimate=pl.CostEstimate(
            flops=2 * all_rows * width * columns,
            bytes_accessed=2 * (2 * all_rows * width + 2 * columns * width),
            transcendentals=0,
        ),
        compiler_params=pltpu.CompilerParams(vmem_limit_bytes=16 * 2**20),
        name="project",
    )(place.reshape(1), *blocks, wd.reshape(pairs, slab, width), kept, came, gains, side)
    got = exchange(partial, MP)
    features_here = lax.optimization_barrier(
        jnp.concatenate([block[:rows] for block in blocks], axis=0)
    )
    summed = jnp.sum(got[:, :mine].astype(jnp.float32), axis=0)
    side = got[:, mine:].reshape(models, 8 * columns)[:, : (kinds + 2) * mine]
    side = side.reshape(models, kinds + 2, mine).astype(jnp.float32)
    peaks = side[:, 0]
    totals = side[:, 1] + side[:, 2]
    moments = side[:, 3] + side[:, 4]
    peak = jnp.max(peaks, axis=0)
    below = peaks - peak
    factor = jnp.exp(below)
    total = jnp.sum(factor * totals, axis=0)
    moment = jnp.sum(factor * (moments + below * totals), axis=0)
    entropy = jnp.log(total) - moment / total
    weight = (side[0, 5] * entropy / math.log(VOCAB)).astype(jnp.bfloat16).astype(jnp.float32)
    square = jnp.sum(side[:, 8] + side[:, 9], axis=0)
    inverse = lax.rsqrt(square / features + EPSILON)
    error = summed * inverse[:, None]
    loss = 0.5 * weight * jnp.sum(error * error, axis=1) * scale
    slope = (error * (weight * inverse * scale)[:, None]).astype(jnp.bfloat16)
    tail = jnp.concatenate(
        [jnp.stack(halves(loss)), side[0, 6:8].astype(jnp.bfloat16)], axis=0
    )
    tail = jnp.pad(tail, ((0, 4), (0, columns - mine)))
    got = spread(jnp.concatenate([slope, tail], axis=0), MP)
    slope = got[:, :mine].reshape(all_rows, columns)
    tail = got[:, mine : mine + 4, :mine].swapaxes(0, 1).reshape(4, all_rows)
    grad = lax.dot_general(
        slope, features_here, (((0,), (0,)), ((), ())), preferred_element_type=jnp.float32
    )
    gain = jnp.sum(grad * wd.astype(jnp.float32), axis=0)

    named = tail[2][None, :] == jnp.arange(groups, dtype=jnp.bfloat16)[:, None]
    block = jnp.arange(all_rows, dtype=jnp.int32) // rows
    quad = 2 * (a ^ (block % 2)) + (zl ^ (block // 2))
    place = quad * CAP + tail[3].astype(jnp.int32)
    there = place[:, None] == jnp.arange(128, dtype=jnp.int32)[None, :]
    zero = jnp.zeros((), jnp.bfloat16)
    named = named.astype(jnp.bfloat16)
    slots = jnp.dot(
        jnp.concatenate([named, named], axis=1),
        jnp.concatenate(
            [jnp.where(there, tail[0][:, None], zero), jnp.where(there, tail[1][:, None], zero)],
            axis=0,
        ),
        preferred_element_type=jnp.float32,
    )
    slots = slots.reshape(2, pairs, 2, 128)

    def toward(swap_a, swap_zl):
        for_them = lax.dynamic_index_in_dim(slots, a ^ swap_a, axis=0, keepdims=False)
        for_them = lax.dynamic_index_in_dim(for_them, zl ^ swap_zl, axis=1, keepdims=False)
        return jnp.concatenate([for_them, gain.reshape(width // 128, 128)], axis=0)

    small = toward(0, 0)
    small += flipped(toward(0, 1), ("zl",))
    small += flipped(toward(1, 0), ("a",))
    small += flipped(toward(1, 1), ("a", "zl"))
    gain_halves = [half.reshape(1, width) for half in halves(small[pairs:])]
    extra = jnp.broadcast_to(jnp.concatenate(gain_halves)[None], (pairs, 2, width))
    slot_halves = jnp.concatenate(halves(small[:pairs]), axis=1)[:, None]
    extra = jnp.concatenate([extra, jnp.pad(slot_halves, ((0, 0), (0, 0), (0, width - 256)))], axis=1)
    extra = jnp.pad(extra, ((0, 0), (0, 5), (0, 0)))
    parts = exchange(
        jnp.concatenate([grad.astype(jnp.bfloat16).reshape(pairs, slab, width), extra], axis=1),
        "zh",
    )
    spread_gain = lax.optimization_barrier(jnp.broadcast_to(draft_gain, (slab, width)) + 0.0)
    grad_weight = jnp.sum(parts[:, :slab].astype(jnp.float32), axis=0) * spread_gain
    extra = parts[:, slab : slab + 3].astype(jnp.float32)
    grad_gain = jnp.sum(extra[:, :2], axis=(0, 1))
    slots = extra[:, 2, : quads * CAP] + extra[:, 2, 128 : 128 + quads * CAP]
    slots = slots.reshape(pairs, 2, 2, CAP).transpose(1, 0, 2, 3)
    return (grad_weight, grad_gain, slots.reshape(groups * CAP))


def solution(mesh):
    fine = Mesh(mesh.devices.reshape(2, 8, 2, 4, 2, 2), DP + MP)
    in_specs = (
        P(DP, MP),
        P(),
        P(MP, None),
        P(MP),
        P(DP, MP),
        P(DP, MP),
        P(DP, None),
        P(DP),
        P(DP, None),
    )
    out_specs = (P(DP, MP), P(MP), P(DP))

    return jax.shard_map(
        on_device, mesh=fine, in_specs=in_specs, out_specs=out_specs, check_vma=False
    )
```

```python
import math

import jax
import jax.numpy as jnp
from jax import lax
from jax.experimental import pallas as pl
from jax.experimental.pallas import tpu as pltpu
from jax.sharding import Mesh, PartitionSpec as P


VOCAB = 32000
LEN = 128
CAP = 10
EPSILON = 1e-05
DP = ("a", "zh", "zl")
MP = ("x", "b", "c")


def exchange(value, axes):
    return lax.all_to_all(value, axes, split_axis=0, concat_axis=0, tiled=True)


def spread(value, axes):
    copies = lax.axis_size(axes)
    return exchange(jnp.broadcast_to(value[None], (copies,) + value.shape), axes)


def halves(value):
    high = value.astype(jnp.bfloat16)
    low = (value - high.astype(jnp.float32)).astype(jnp.bfloat16)
    return high, low


def flipped(value, axes):
    sizes = [lax.axis_size(axis) for axis in axes]
    last = math.prod(sizes) - 1
    return lax.ppermute(value, axes, [(k, last - k) for k in range(last + 1)])


def teacher_block(target_weight, a, zl, slab, width):
    x, b, c = (lax.axis_index(axis) for axis in MP)
    quarter = 4 * width

    def piece(column):
        return lax.dynamic_slice(target_weight, (zl * slab, column * quarter), (slab, quarter))

    def turn(swap):
        moves = []
        for k in range(8):
            side, at = divmod(k, 4)
            moves.append((k, at // 2 * 4 + 2 * side + (at % 2) ^ swap))
        return moves

    near = lax.ppermute(piece(2 * a + x % 2), ("a", "x"), turn(0))
    far = lax.ppermute(piece(2 * a + 1 - x % 2), ("a", "x"), turn(1))

    def halve(parts, mine, axis):
        half = parts[0].shape[1] // 2

        def side(which):
            return jnp.concatenate(
                [lax.dynamic_slice_in_dim(part, which * half, half, axis=1) for part in parts]
            )

        return side(mine), flipped(side(1 - mine), (axis,))

    parts = halve((near, far), b, "b")
    parts = halve(parts, c, "c")
    return [part.reshape(4, slab, width) for part in parts], 4 * (x % 2) + 2 * b + c


def project(place, own, across, beside, both, wd, kept, came, gains, side, out):
    slab = wd.shape[1]
    mine = out.shape[1] - side.shape[1]
    here = place[0]
    draft_gain, target_gain = gains[0:1], gains[1:2]
    for pair in range(4):
        merged = []
        for k in (2 * pair, 2 * pair + 1):
            away = here ^ k
            at = away // 2 % 2 * 2 + away // 4
            parts = kept[at], came[at]
            wt = jnp.where(away % 2 == 1, parts[1].astype(jnp.float32), parts[0].astype(jnp.float32))
            merged.append(wd[k].astype(jnp.float32) * draft_gain - wt * target_gain)
        merged = jnp.concatenate(merged).astype(jnp.bfloat16)
        lanes = slice(pair * 2 * slab, (pair + 1) * 2 * slab)
        for quad, block in enumerate((own, across, beside, both)):
            value = lax.dot_general(
                block[: 4 * mine],
                merged,
                (((1,), (1,)), ((), ())),
                preferred_element_type=jnp.float32,
            )
            out[4 * quad : 4 * quad + 4, :mine, lanes] = value.astype(jnp.bfloat16).reshape(
                4, mine, 2 * slab
            )
    out[:, mine:] = side[...]


def softmax_parts(logit_rows):
    values = logit_rows.astype(jnp.float32)
    highest = jnp.max(values, axis=1)
    shifted = values - highest[:, None]
    expsum = jnp.exp(shifted)
    return highest, jnp.sum(expsum, axis=1), jnp.sum(expsum * shifted, axis=1)


def on_device(
    hidden,
    target_gain,
    target_weight,
    draft_gain,
    draft_weight,
    logits,
    seq_lens,
    tool_mask,
    owners,
):
    rows, width = hidden.shape
    features = target_gain.shape[0]
    models = lax.axis_size(MP)
    groups = lax.axis_size(DP)
    pairs = lax.axis_size("zh")
    quads = groups // pairs
    slab = draft_weight.shape[0]
    columns = pairs * slab
    all_rows = quads * rows
    mine = all_rows // models
    a, zl = lax.axis_index("a"), lax.axis_index("zl")
    model = lax.axis_index(MP)
    scale = 1.0 / math.sqrt(rows * groups)

    index = jnp.arange(rows, dtype=jnp.int32)
    length = jnp.where(index < LEN, seq_lens[0, 0], seq_lens[0, 1])
    valid = jnp.logical_and(index % LEN < length - 1, tool_mask == 1)
    owner = owners[:, 0]
    earlier = jnp.logical_and(
        owner[:, None] == owner[None, :], index[:, None] < index[None, :]
    )
    rank = jnp.sum(earlier.astype(jnp.int32), axis=0)
    highest, total, moment = softmax_parts(logits)
    total_high, total_low = halves(total)
    moment_high, moment_low = halves(moment)
    facts = jnp.stack(
        [
            highest.astype(jnp.bfloat16),
            total_high,
            total_low,
            moment_high,
            moment_low,
            valid.astype(jnp.bfloat16),
            owner.astype(jnp.bfloat16),
            rank.astype(jnp.bfloat16),
        ]
    )
    kinds = facts.shape[0]

    wd = spread(draft_weight, "zh").reshape(columns, width)
    own = jnp.concatenate([hidden, jnp.pad(facts, ((0, 0), (0, width - rows)))], axis=0)
    across = flipped(own, ("a",))
    beside = flipped(own, ("zl",))
    both = flipped(across, ("zl",))
    blocks = (own, across, beside, both)
    facts_here = jnp.stack([block[rows:, :rows] for block in blocks])
    (kept, came), place = teacher_block(target_weight, a, zl, slab, width)

    gain_slice = lax.dynamic_slice_in_dim(target_gain, model * width, width)
    gains = jnp.stack([draft_gain, gain_slice])
    squares = [jnp.sum(block[:rows].astype(jnp.float32) ** 2, axis=1) for block in blocks]
    squares = jnp.stack(halves(jnp.stack(squares))).reshape(2, models, mine)
    facts_here = facts_here.swapaxes(0, 1).reshape(kinds, models, mine)
    side = jnp.concatenate([facts_here, squares], axis=0).swapaxes(0, 1)
    side = side.reshape(models, 1, (kinds + 2) * mine)
    side = jnp.pad(side, ((0, 0), (0, 0), (0, 8 * columns - side.shape[2]))).reshape(models, 8, columns)
    partial = pl.pallas_call(
        project,
        out_shape=jax.ShapeDtypeStruct((models, mine + 8, columns), jnp.bfloat16),
        in_specs=[pl.BlockSpec(memory_space=pltpu.SMEM)]
        + [pl.BlockSpec(memory_space=pltpu.VMEM)] * 9,
        out_specs=pl.BlockSpec(memory_space=pltpu.VMEM),
        cost_estimate=pl.CostEstimate(
            flops=2 * all_rows * width * columns,
            bytes_accessed=2 * (2 * all_rows * width + 2 * columns * width),
            transcendentals=0,
        ),
        compiler_params=pltpu.CompilerParams(vmem_limit_bytes=16 * 2**20),
        name="project",
    )(place.reshape(1), *blocks, wd.reshape(pairs, slab, width), kept, came, gains, side)
    got = exchange(partial, MP)
    features_here = lax.optimization_barrier(
        jnp.concatenate([block[:rows] for block in blocks], axis=0)
    )
    summed = jnp.sum(got[:, :mine].astype(jnp.float32), axis=0)
    side = got[:, mine:].reshape(models, 8 * columns)[:, : (kinds + 2) * mine]
    side = side.reshape(models, kinds + 2, mine).astype(jnp.float32)
    peaks = side[:, 0]
    totals = side[:, 1] + side[:, 2]
    moments = side[:, 3] + side[:, 4]
    peak = jnp.max(peaks, axis=0)
    below = peaks - peak
    factor = jnp.exp(below)
    total = jnp.sum(factor * totals, axis=0)
    moment = jnp.sum(factor * (moments + below * totals), axis=0)
    entropy = jnp.log(total) - moment / total
    weight = (side[0, 5] * entropy / math.log(VOCAB)).astype(jnp.bfloat16).astype(jnp.float32)
    square = jnp.sum(side[:, 8] + side[:, 9], axis=0)
    inverse = lax.rsqrt(square / features + EPSILON)
    error = summed * inverse[:, None]
    loss = 0.5 * weight * jnp.sum(error * error, axis=1) * scale
    slope = (error * (weight * inverse * scale)[:, None]).astype(jnp.bfloat16)
    tail = jnp.concatenate(
        [jnp.stack(halves(loss)), side[0, 6:8].astype(jnp.bfloat16)], axis=0
    )
    tail = jnp.pad(tail, ((0, 4), (0, columns - mine)))
    got = spread(jnp.concatenate([slope, tail], axis=0), MP)
    slope = got[:, :mine].reshape(all_rows, columns)
    tail = got[:, mine : mine + 4, :mine].swapaxes(0, 1).reshape(4, all_rows)
    grad = lax.dot_general(
        slope, features_here, (((0,), (0,)), ((), ())), preferred_element_type=jnp.float32
    )
    gain = jnp.sum(grad * wd.astype(jnp.float32), axis=0)

    named = tail[2][None, :] == jnp.arange(groups, dtype=jnp.bfloat16)[:, None]
    block = jnp.arange(all_rows, dtype=jnp.int32) // rows
    quad = 2 * (a ^ (block % 2)) + (zl ^ (block // 2))
    place = quad * CAP + tail[3].astype(jnp.int32)
    there = place[:, None] == jnp.arange(128, dtype=jnp.int32)[None, :]
    zero = jnp.zeros((), jnp.bfloat16)
    named = named.astype(jnp.bfloat16)
    slots = jnp.dot(
        jnp.concatenate([named, named], axis=1),
        jnp.concatenate(
            [jnp.where(there, tail[0][:, None], zero), jnp.where(there, tail[1][:, None], zero)],
            axis=0,
        ),
        preferred_element_type=jnp.float32,
    )
    slots = slots.reshape(2, pairs, 2, 128).transpose(0, 2, 1, 3).reshape(quads, pairs, 128)
    gain = jnp.broadcast_to(gain.reshape(1, width // 128, 128), (quads, width // 128, 128))
    small = jnp.concatenate([slots, gain, jnp.zeros((quads, 4, 128), jnp.float32)], axis=1)
    small = jnp.sum(exchange(small, ("a", "zl")), axis=0)
    small = small[: pairs + width // 128]
    gain_halves = [half.reshape(1, width) for half in halves(small[pairs:])]
    extra = jnp.broadcast_to(jnp.concatenate(gain_halves)[None], (pairs, 2, width))
    slot_halves = jnp.concatenate(halves(small[:pairs]), axis=1)[:, None]
    extra = jnp.concatenate([extra, jnp.pad(slot_halves, ((0, 0), (0, 0), (0, width - 256)))], axis=1)
    extra = jnp.pad(extra, ((0, 0), (0, 5), (0, 0)))
    parts = exchange(
        jnp.concatenate([grad.astype(jnp.bfloat16).reshape(pairs, slab, width), extra], axis=1),
        "zh",
    )
    spread_gain = lax.optimization_barrier(jnp.broadcast_to(draft_gain, (slab, width)) + 0.0)
    grad_weight = jnp.sum(parts[:, :slab].astype(jnp.float32), axis=0) * spread_gain
    extra = parts[:, slab : slab + 3].astype(jnp.float32)
    grad_gain = jnp.sum(extra[:, :2], axis=(0, 1))
    slots = extra[:, 2, : quads * CAP] + extra[:, 2, 128 : 128 + quads * CAP]
    slots = slots.reshape(pairs, 2, 2, CAP).transpose(1, 0, 2, 3)
    return (grad_weight, grad_gain, slots.reshape(groups * CAP))


def solution(mesh):
    fine = Mesh(mesh.devices.reshape(2, 8, 2, 4, 2, 2), DP + MP)
    in_specs = (
        P(DP, MP),
        P(),
        P(MP, None),
        P(MP),
        P(DP, MP),
        P(DP, MP),
        P(DP, None),
        P(DP),
        P(DP, None),
    )
    out_specs = (P(DP, MP), P(MP), P(DP))

    return jax.shard_map(
        on_device, mesh=fine, in_specs=in_specs, out_specs=out_specs, check_vma=False
    )
```

```python
import math

import jax
import jax.numpy as jnp
from jax import lax
from jax.experimental import pallas as pl
from jax.experimental.pallas import tpu as pltpu
from jax.sharding import Mesh, PartitionSpec as P


VOCAB = 32000
LEN = 128
CAP = 10
EPSILON = 1e-05
DP = ("a", "zh", "zl")
MP = ("x", "b", "c")


def exchange(value, axes):
    return lax.all_to_all(value, axes, split_axis=0, concat_axis=0, tiled=True)


def spread(value, axes):
    copies = lax.axis_size(axes)
    return exchange(jnp.broadcast_to(value[None], (copies,) + value.shape), axes)


def halves(value):
    high = value.astype(jnp.bfloat16)
    low = (value - high.astype(jnp.float32)).astype(jnp.bfloat16)
    return high, low


def flipped(value, axes):
    sizes = [lax.axis_size(axis) for axis in axes]
    last = math.prod(sizes) - 1
    return lax.ppermute(value, axes, [(k, last - k) for k in range(last + 1)])


def teacher_block(target_weight, a, zl, slab, width):
    x, b, c = (lax.axis_index(axis) for axis in MP)
    quarter = 4 * width

    def piece(column):
        return lax.dynamic_slice(target_weight, (zl * slab, column * quarter), (slab, quarter))

    def turn(swap):
        moves = []
        for k in range(8):
            side, at = divmod(k, 4)
            moves.append((k, at // 2 * 4 + 2 * side + (at % 2) ^ swap))
        return moves

    near = lax.ppermute(piece(2 * a + x % 2), ("a", "x"), turn(0))
    far = lax.ppermute(piece(2 * a + 1 - x % 2), ("a", "x"), turn(1))

    def halve(parts, mine, axis):
        half = parts[0].shape[1] // 2

        def side(which):
            return jnp.concatenate(
                [lax.dynamic_slice_in_dim(part, which * half, half, axis=1) for part in parts]
            )

        return side(mine), flipped(side(1 - mine), (axis,))

    parts = halve((near, far), b, "b")
    parts = halve(parts, c, "c")
    return [part.reshape(4, slab, width) for part in parts], 4 * (x % 2) + 2 * b + c


LANES = 128


def project(place, own, across, beside, both, wd, kept, came, gains, side, out):
    slab = wd.shape[1]
    mine = (out.shape[1] - side.shape[1]) // 4
    here = place[0]
    draft_gain, target_gain = gains[0:1], gains[1:2]
    for pair in range(4):
        merged = []
        for k in (2 * pair, 2 * pair + 1):
            away = here ^ k
            at = away // 2 % 2 * 2 + away // 4
            parts = kept[at], came[at]
            wt = jnp.where(away % 2 == 1, parts[1].astype(jnp.float32), parts[0].astype(jnp.float32))
            merged.append(wd[k].astype(jnp.float32) * draft_gain - wt * target_gain)
        merged = jnp.concatenate(merged).astype(jnp.bfloat16)
        for quad, block in enumerate((own, across, beside, both)):
            value = lax.dot_general(
                block[: 4 * mine],
                merged,
                (((1,), (1,)), ((), ())),
                preferred_element_type=jnp.float32,
            )
            out[4 * quad : 4 * quad + 4, pair * mine : (pair + 1) * mine] = value.astype(
                jnp.bfloat16
            ).reshape(4, mine, 2 * slab)
    out[:, 4 * mine :] = side[...]


def backward(got, own, across, beside, both, wd, out, gain):
    _, slab, width = wd.shape
    mine = slab
    total = jnp.zeros((1, width), jnp.float32)
    for chunk in range(4):
        grad = jnp.zeros((LANES, width), jnp.float32)
        for quad, block in enumerate((own, across, beside, both)):
            slope = got[4 * quad : 4 * quad + 4, chunk * mine : (chunk + 1) * mine]
            grad += lax.dot_general(
                slope.reshape(4 * mine, LANES),
                block[: 4 * mine],
                (((0,), (0,)), ((), ())),
                preferred_element_type=jnp.float32,
            )
        for k in range(2):
            rows = grad[k * slab : (k + 1) * slab]
            total += jnp.sum(rows * wd[2 * chunk + k].astype(jnp.float32), axis=0, keepdims=True)
            for part in range(width // LANES):
                out[2 * chunk + k, part * slab : (part + 1) * slab] = rows[
                    :, part * LANES : (part + 1) * LANES
                ].astype(jnp.bfloat16)
    gain[...] = total


def on_chip(kernel, out_shape, flops, moved, *args, scalars=0):
    space = [pl.BlockSpec(memory_space=pltpu.SMEM)] * scalars
    space += [pl.BlockSpec(memory_space=pltpu.VMEM)] * (len(args) - scalars)
    return pl.pallas_call(
        kernel,
        out_shape=out_shape,
        in_specs=space,
        out_specs=jax.tree.map(lambda _: pl.BlockSpec(memory_space=pltpu.VMEM), out_shape),
        cost_estimate=pl.CostEstimate(flops=flops, bytes_accessed=moved, transcendentals=0),
        compiler_params=pltpu.CompilerParams(vmem_limit_bytes=16 * 2**20),
    )(*args)


def spread_gain(part, slab):
    part = part.reshape(-1, 1, LANES)
    return lax.optimization_barrier(jnp.broadcast_to(part, (part.shape[0], slab, LANES)))


def softmax_parts(logit_rows):
    values = logit_rows.astype(jnp.float32)
    highest = jnp.max(values, axis=1)
    shifted = values - highest[:, None]
    expsum = jnp.exp(shifted)
    return highest, jnp.sum(expsum, axis=1), jnp.sum(expsum * shifted, axis=1)


def on_device(
    hidden,
    target_gain,
    target_weight,
    draft_gain,
    draft_weight,
    logits,
    seq_lens,
    tool_mask,
    owners,
):
    rows, width = hidden.shape
    features = target_gain.shape[0]
    models = lax.axis_size(MP)
    groups = lax.axis_size(DP)
    pairs = lax.axis_size("zh")
    quads = groups // pairs
    slab = draft_weight.shape[0]
    columns = pairs * slab
    all_rows = quads * rows
    mine = all_rows // models
    a, zl = lax.axis_index("a"), lax.axis_index("zl")
    model = lax.axis_index(MP)
    scale = 1.0 / math.sqrt(rows * groups)

    index = jnp.arange(rows, dtype=jnp.int32)
    length = jnp.where(index < LEN, seq_lens[0, 0], seq_lens[0, 1])
    valid = jnp.logical_and(index % LEN < length - 1, tool_mask == 1)
    owner = owners[:, 0]
    earlier = jnp.logical_and(
        owner[:, None] == owner[None, :], index[:, None] < index[None, :]
    )
    rank = jnp.sum(earlier.astype(jnp.int32), axis=0)
    highest, total, moment = softmax_parts(logits)
    total_high, total_low = halves(total)
    moment_high, moment_low = halves(moment)
    facts = jnp.stack(
        [
            highest.astype(jnp.bfloat16),
            total_high,
            total_low,
            moment_high,
            moment_low,
            valid.astype(jnp.bfloat16),
            owner.astype(jnp.bfloat16),
            rank.astype(jnp.bfloat16),
        ]
    )
    kinds = facts.shape[0]

    wd = spread(draft_weight, "zh").reshape(columns, width)
    own = jnp.concatenate([hidden, jnp.pad(facts, ((0, 0), (0, width - rows)))], axis=0)
    across = flipped(own, ("a",))
    beside = flipped(own, ("zl",))
    both = flipped(across, ("zl",))
    blocks = (own, across, beside, both)
    facts_here = jnp.stack([block[rows:, :rows] for block in blocks])
    (kept, came), place = teacher_block(target_weight, a, zl, slab, width)

    gain_slice = lax.dynamic_slice_in_dim(target_gain, model * width, width)
    gains = jnp.stack([draft_gain, gain_slice])
    squares = [jnp.sum(block[:rows].astype(jnp.float32) ** 2, axis=1) for block in blocks]
    squares = jnp.stack(halves(jnp.stack(squares))).reshape(2, models, mine)
    facts_here = facts_here.swapaxes(0, 1).reshape(kinds, models, mine)
    side = jnp.concatenate([facts_here, squares], axis=0).swapaxes(0, 1)
    side = side.reshape(models, (kinds + 2) * mine // LANES, LANES)
    side = jnp.pad(side, ((0, 0), (0, 8 - side.shape[1]), (0, 0)))
    held = columns // LANES * mine
    flops = 2 * all_rows * width * columns
    moved = 2 * (2 * all_rows * width + 2 * columns * width)
    wd = wd.reshape(pairs, slab, width)
    partial = on_chip(
        project,
        jax.ShapeDtypeStruct((models, held + 8, LANES), jnp.bfloat16),
        flops,
        moved,
        *(place.reshape(1), *blocks, wd, kept, came, gains, side),
        scalars=1,
    )
    got = exchange(partial, MP)
    first_gain = spread_gain(draft_gain[: width // 2], slab)
    summed = jnp.sum(got[:, :held].astype(jnp.float32), axis=0).reshape(held // mine, mine, LANES)
    side = got[:, held : held + (kinds + 2) * mine // LANES]
    side = side.reshape(models, kinds + 2, mine).astype(jnp.float32)
    peaks = side[:, 0]
    totals = side[:, 1] + side[:, 2]
    moments = side[:, 3] + side[:, 4]
    peak = jnp.max(peaks, axis=0)
    below = peaks - peak
    factor = jnp.exp(below)
    total = jnp.sum(factor * totals, axis=0)
    moment = jnp.sum(factor * (moments + below * totals), axis=0)
    entropy = jnp.log(total) - moment / total
    weight = (side[0, 5] * entropy / math.log(VOCAB)).astype(jnp.bfloat16).astype(jnp.float32)
    square = jnp.sum(side[:, 8] + side[:, 9], axis=0)
    inverse = lax.rsqrt(square / features + EPSILON)
    error = summed * inverse[None, :, None]
    loss = 0.5 * weight * jnp.sum(error * error, axis=(0, 2)) * scale
    slope = (error * (weight * inverse * scale)[None, :, None]).astype(jnp.bfloat16)
    tail = jnp.concatenate(
        [jnp.stack(halves(loss)), side[0, 6:8].astype(jnp.bfloat16)], axis=0
    ).reshape(4 * mine // LANES, LANES)
    tail = jnp.pad(tail, ((0, 8 - tail.shape[0]), (0, 0)))
    got = spread(jnp.concatenate([slope.reshape(held, LANES), tail], axis=0), MP)
    tail = got[:, held : held + 4 * mine // LANES].reshape(models, 4, mine)
    tail = tail.swapaxes(0, 1).reshape(4, all_rows)
    grad, gain = on_chip(
        backward,
        (
            jax.ShapeDtypeStruct((pairs, width // LANES * slab, LANES), jnp.bfloat16),
            jax.ShapeDtypeStruct((1, width), jnp.float32),
        ),
        flops,
        moved,
        *(got, *blocks, wd),
    )

    named = tail[2][None, :] == jnp.arange(groups, dtype=jnp.bfloat16)[:, None]
    block = jnp.arange(all_rows, dtype=jnp.int32) // rows
    quad = 2 * (a ^ (block % 2)) + (zl ^ (block // 2))
    place = quad * CAP + tail[3].astype(jnp.int32)
    there = place[:, None] == jnp.arange(128, dtype=jnp.int32)[None, :]
    zero = jnp.zeros((), jnp.bfloat16)
    named = named.astype(jnp.bfloat16)
    slots = jnp.dot(
        jnp.concatenate([named, named], axis=1),
        jnp.concatenate(
            [jnp.where(there, tail[0][:, None], zero), jnp.where(there, tail[1][:, None], zero)],
            axis=0,
        ),
        preferred_element_type=jnp.float32,
    )
    slots = slots.reshape(2, pairs, 2, 128).transpose(0, 2, 1, 3).reshape(quads, pairs, 128)
    gain = jnp.broadcast_to(gain.reshape(1, width // 128, 128), (quads, width // 128, 128))
    small = jnp.concatenate([slots, gain, jnp.zeros((quads, 4, 128), jnp.float32)], axis=1)
    small = jnp.sum(exchange(small, ("a", "zl")), axis=0)
    small = small[: pairs + width // 128]
    sent_gain = jnp.broadcast_to(
        small[pairs:].astype(jnp.bfloat16)[None], (pairs, width // LANES, LANES)
    )
    sent_slots = jnp.concatenate([half[:, :64] for half in halves(small[:pairs])], axis=1)
    extra = jnp.concatenate([sent_gain, sent_slots[:, None]], axis=1)
    extra = jnp.pad(extra, ((0, 0), (0, 8 - extra.shape[1]), (0, 0)))
    parts = exchange(jnp.concatenate([grad, extra], axis=1), "zh")
    last_gain = spread_gain(draft_gain[width // 2 :], slab)
    chunks = width // LANES
    grad_weight = jnp.sum(parts[:, : chunks * slab].astype(jnp.float32), axis=0)
    grad_weight = grad_weight.reshape(chunks, slab, LANES)
    grad_weight *= jnp.concatenate([first_gain, last_gain], axis=0)
    grad_weight = grad_weight.swapaxes(0, 1).reshape(slab, width)
    extra = parts[:, chunks * slab :].astype(jnp.float32)
    grad_gain = jnp.sum(extra[:, :chunks], axis=0).reshape(width)
    slots = extra[:, chunks, : quads * CAP] + extra[:, chunks, 64 : 64 + quads * CAP]
    slots = slots.reshape(pairs, 2, 2, CAP).transpose(1, 0, 2, 3)
    return (grad_weight, grad_gain, slots.reshape(groups * CAP))


def solution(mesh):
    fine = Mesh(mesh.devices.reshape(2, 8, 2, 4, 2, 2), DP + MP)
    in_specs = (
        P(DP, MP),
        P(),
        P(MP, None),
        P(MP),
        P(DP, MP),
        P(DP, MP),
        P(DP, None),
        P(DP),
        P(DP, None),
    )
    out_specs = (P(DP, MP), P(MP), P(DP))

    return jax.shard_map(
        on_device, mesh=fine, in_specs=in_specs, out_specs=out_specs, check_vma=False
    )
```

```python
import math

import jax
import jax.numpy as jnp
from jax import lax
from jax.experimental import pallas as pl
from jax.experimental.pallas import tpu as pltpu
from jax.sharding import Mesh, PartitionSpec as P


VOCAB = 32000
LEN = 128
CAP = 10
EPSILON = 1e-05
DP = ("a", "zh", "zl")
MP = ("x", "b", "c")


def exchange(value, axes):
    return lax.all_to_all(value, axes, split_axis=0, concat_axis=0, tiled=True)


def spread(value, axes):
    copies = lax.axis_size(axes)
    return exchange(jnp.broadcast_to(value[None], (copies,) + value.shape), axes)


def halves(value):
    high = value.astype(jnp.bfloat16)
    low = (value - high.astype(jnp.float32)).astype(jnp.bfloat16)
    return high, low


def flipped(value, axes):
    sizes = [lax.axis_size(axis) for axis in axes]
    last = math.prod(sizes) - 1
    return lax.ppermute(value, axes, [(k, last - k) for k in range(last + 1)])


def teacher_block(target_weight, a, zl, slab, width):
    x, b, c = (lax.axis_index(axis) for axis in MP)
    quarter = 4 * width

    def piece(column):
        return lax.dynamic_slice(target_weight, (zl * slab, column * quarter), (slab, quarter))

    def turn(swap):
        moves = []
        for k in range(8):
            side, at = divmod(k, 4)
            moves.append((k, at // 2 * 4 + 2 * side + (at % 2) ^ swap))
        return moves

    near = lax.ppermute(piece(2 * a + x % 2), ("a", "x"), turn(0))
    far = lax.ppermute(piece(2 * a + 1 - x % 2), ("a", "x"), turn(1))

    def halve(parts, mine, axis):
        half = parts[0].shape[1] // 2

        def side(which):
            return jnp.concatenate(
                [lax.dynamic_slice_in_dim(part, which * half, half, axis=1) for part in parts]
            )

        return side(mine), flipped(side(1 - mine), (axis,))

    parts = halve((near, far), b, "b")
    parts = halve(parts, c, "c")
    return [part.reshape(4, slab, width) for part in parts], 4 * (x % 2) + 2 * b + c


LANES = 128


def project(place, own, across, beside, both, wd, kept, came, gains, side, out):
    slab = wd.shape[1]
    mine = (out.shape[1] - side.shape[1]) // 4
    here = place[0]
    draft_gain, target_gain = gains[0:1], gains[1:2]
    for pair in range(4):
        merged = []
        for k in (2 * pair, 2 * pair + 1):
            away = here ^ k
            at = away // 2 % 2 * 2 + away // 4
            parts = kept[at], came[at]
            wt = jnp.where(away % 2 == 1, parts[1].astype(jnp.float32), parts[0].astype(jnp.float32))
            merged.append(wd[k].astype(jnp.float32) * draft_gain - wt * target_gain)
        merged = jnp.concatenate(merged).astype(jnp.bfloat16)
        for quad, block in enumerate((own, across, beside, both)):
            value = lax.dot_general(
                block[: 4 * mine],
                merged,
                (((1,), (1,)), ((), ())),
                preferred_element_type=jnp.float32,
            )
            out[4 * quad : 4 * quad + 4, pair * mine : (pair + 1) * mine] = value.astype(
                jnp.bfloat16
            ).reshape(4, mine, 2 * slab)
    out[:, 4 * mine :] = side[...]


def backward(got, own, across, beside, both, wd, out, gain):
    _, slab, width = wd.shape
    mine = slab
    total = jnp.zeros((1, width), jnp.float32)
    for chunk in range(4):
        grad = jnp.zeros((LANES, width), jnp.float32)
        for quad, block in enumerate((own, across, beside, both)):
            slope = got[4 * quad : 4 * quad + 4, chunk * mine : (chunk + 1) * mine]
            grad += lax.dot_general(
                slope.reshape(4 * mine, LANES),
                block[: 4 * mine],
                (((0,), (0,)), ((), ())),
                preferred_element_type=jnp.float32,
            )
        for k in range(2):
            rows = grad[k * slab : (k + 1) * slab]
            total += jnp.sum(rows * wd[2 * chunk + k].astype(jnp.float32), axis=0, keepdims=True)
            for part in range(width // LANES):
                out[2 * chunk + k, part * slab : (part + 1) * slab] = rows[
                    :, part * LANES : (part + 1) * LANES
                ].astype(jnp.bfloat16)
    gain[...] = total


def finish(parts, first_gain, last_gain, grad, gain, slots):
    pairs = parts.shape[0]
    slab, width = grad.shape
    chunks = width // LANES
    for chunk in range(chunks):
        total = parts[0, chunk * slab : (chunk + 1) * slab].astype(jnp.float32)
        for k in range(1, pairs):
            total += parts[k, chunk * slab : (chunk + 1) * slab].astype(jnp.float32)
        held = first_gain if chunk < chunks // 2 else last_gain
        grad[:, chunk * LANES : (chunk + 1) * LANES] = total * held[chunk % (chunks // 2), 0:1]
    total = parts[0, chunks * slab :].astype(jnp.float32)
    slots[0:1] = total[chunks : chunks + 1]
    for k in range(1, pairs):
        extra = parts[k, chunks * slab :].astype(jnp.float32)
        slots[k : k + 1] = extra[chunks : chunks + 1]
        total += extra
    gain[...] = total[:chunks]


def on_chip(kernel, out_shape, flops, moved, *args, scalars=0):
    space = [pl.BlockSpec(memory_space=pltpu.SMEM)] * scalars
    space += [pl.BlockSpec(memory_space=pltpu.VMEM)] * (len(args) - scalars)
    return pl.pallas_call(
        kernel,
        out_shape=out_shape,
        in_specs=space,
        out_specs=jax.tree.map(lambda _: pl.BlockSpec(memory_space=pltpu.VMEM), out_shape),
        cost_estimate=pl.CostEstimate(flops=flops, bytes_accessed=moved, transcendentals=0),
        compiler_params=pltpu.CompilerParams(vmem_limit_bytes=16 * 2**20),
    )(*args)


def spread_gain(part):
    part = part.reshape(-1, 1, LANES)
    return lax.optimization_barrier(jnp.broadcast_to(part, (part.shape[0], 8, LANES)))


def softmax_parts(logit_rows):
    values = logit_rows.astype(jnp.float32)
    highest = jnp.max(values, axis=1)
    shifted = values - highest[:, None]
    expsum = jnp.exp(shifted)
    return highest, jnp.sum(expsum, axis=1), jnp.sum(expsum * shifted, axis=1)


def on_device(
    hidden,
    target_gain,
    target_weight,
    draft_gain,
    draft_weight,
    logits,
    seq_lens,
    tool_mask,
    owners,
):
    rows, width = hidden.shape
    features = target_gain.shape[0]
    models = lax.axis_size(MP)
    groups = lax.axis_size(DP)
    pairs = lax.axis_size("zh")
    quads = groups // pairs
    slab = draft_weight.shape[0]
    columns = pairs * slab
    all_rows = quads * rows
    mine = all_rows // models
    a, zl = lax.axis_index("a"), lax.axis_index("zl")
    model = lax.axis_index(MP)
    scale = 1.0 / math.sqrt(rows * groups)

    index = jnp.arange(rows, dtype=jnp.int32)
    position = jnp.arange(LEN, dtype=jnp.int32)[None, :]
    reached = position < seq_lens[0][:, None] - 1
    valid = jnp.logical_and(reached, tool_mask.reshape(-1, LEN) == 1).reshape(rows)
    owner = owners[:, 0]
    earlier = jnp.logical_and(
        owner[:, None] == owner[None, :], index[:, None] < index[None, :]
    )
    rank = jnp.sum(earlier.astype(jnp.int32), axis=0)
    highest, total, moment = softmax_parts(logits)
    total_high, total_low = halves(total)
    moment_high, moment_low = halves(moment)
    facts = jnp.stack(
        [
            highest.astype(jnp.bfloat16),
            total_high,
            total_low,
            moment_high,
            moment_low,
            valid.astype(jnp.bfloat16),
            owner.astype(jnp.bfloat16),
            rank.astype(jnp.bfloat16),
        ]
    )
    kinds = facts.shape[0]

    wd = spread(draft_weight, "zh").reshape(columns, width)
    own = jnp.concatenate([hidden, jnp.pad(facts, ((0, 0), (0, width - rows)))], axis=0)
    across = flipped(own, ("a",))
    beside = flipped(own, ("zl",))
    both = flipped(across, ("zl",))
    blocks = (own, across, beside, both)
    facts_here = jnp.stack([block[rows:, :rows] for block in blocks])
    (kept, came), place = teacher_block(target_weight, a, zl, slab, width)

    gain_slice = lax.dynamic_slice_in_dim(target_gain, model * width, width)
    gains = jnp.stack([draft_gain, gain_slice])
    squares = [jnp.sum(block[:rows].astype(jnp.float32) ** 2, axis=1) for block in blocks]
    squares = jnp.stack(halves(jnp.stack(squares))).reshape(2, models, mine)
    facts_here = facts_here.swapaxes(0, 1).reshape(kinds, models, mine)
    side = jnp.concatenate([facts_here, squares], axis=0).swapaxes(0, 1)
    side = side.reshape(models, (kinds + 2) * mine // LANES, LANES)
    side = jnp.pad(side, ((0, 0), (0, 8 - side.shape[1]), (0, 0)))
    held = columns // LANES * mine
    flops = 2 * all_rows * width * columns
    moved = 2 * (2 * all_rows * width + 2 * columns * width)
    wd = wd.reshape(pairs, slab, width)
    partial = on_chip(
        project,
        jax.ShapeDtypeStruct((models, held + 8, LANES), jnp.bfloat16),
        flops,
        moved,
        *(place.reshape(1), *blocks, wd, kept, came, gains, side),
        scalars=1,
    )
    got = exchange(partial, MP)
    first_gain = spread_gain(draft_gain[: width // 2])
    summed = jnp.sum(got[:, :held].astype(jnp.float32), axis=0).reshape(held // mine, mine, LANES)
    side = got[:, held : held + (kinds + 2) * mine // LANES]
    side = side.reshape(models, kinds + 2, mine).astype(jnp.float32)
    peaks = side[:, 0]
    totals = side[:, 1] + side[:, 2]
    moments = side[:, 3] + side[:, 4]
    peak = jnp.max(peaks, axis=0)
    below = peaks - peak
    factor = jnp.exp(below)
    total = jnp.sum(factor * totals, axis=0)
    moment = jnp.sum(factor * (moments + below * totals), axis=0)
    entropy = jnp.log(total) - moment / total
    weight = (side[0, 5] * entropy / math.log(VOCAB)).astype(jnp.bfloat16).astype(jnp.float32)
    square = jnp.sum(side[:, 8] + side[:, 9], axis=0)
    inverse = lax.rsqrt(square / features + EPSILON)
    error = summed * inverse[None, :, None]
    loss = 0.5 * weight * jnp.sum(error * error, axis=(0, 2)) * scale
    slope = (error * (weight * inverse * scale)[None, :, None]).astype(jnp.bfloat16)
    tail = jnp.concatenate(
        [jnp.stack(halves(loss)), side[0, 6:8].astype(jnp.bfloat16)], axis=0
    ).reshape(4 * mine // LANES, LANES)
    tail = jnp.pad(tail, ((0, 8 - tail.shape[0]), (0, 0)))
    got = spread(jnp.concatenate([slope.reshape(held, LANES), tail], axis=0), MP)
    tail = got[:, held : held + 4 * mine // LANES].reshape(models, 4, mine)
    tail = tail.swapaxes(0, 1).reshape(4, all_rows)
    grad, gain = on_chip(
        backward,
        (
            jax.ShapeDtypeStruct((pairs, width // LANES * slab, LANES), jnp.bfloat16),
            jax.ShapeDtypeStruct((1, width), jnp.float32),
        ),
        flops,
        moved,
        *(got, *blocks, wd),
    )

    named = tail[2][None, :] == jnp.arange(groups, dtype=jnp.bfloat16)[:, None]
    block = jnp.arange(all_rows, dtype=jnp.int32) // rows
    quad = 2 * (a ^ (block % 2)) + (zl ^ (block // 2))
    place = quad * CAP + tail[3].astype(jnp.int32)
    there = place[:, None] == jnp.arange(128, dtype=jnp.int32)[None, :]
    zero = jnp.zeros((), jnp.bfloat16)
    named = named.astype(jnp.bfloat16)
    slots = jnp.dot(
        jnp.concatenate([named, named], axis=1),
        jnp.concatenate(
            [jnp.where(there, tail[0][:, None], zero), jnp.where(there, tail[1][:, None], zero)],
            axis=0,
        ),
        preferred_element_type=jnp.float32,
    )
    slots = slots.reshape(2, pairs, 2, 128).transpose(0, 2, 1, 3).reshape(quads, pairs, 128)
    gain = jnp.broadcast_to(gain.reshape(1, width // 128, 128), (quads, width // 128, 128))
    small = jnp.concatenate([slots, gain, jnp.zeros((quads, 4, 128), jnp.float32)], axis=1)
    small = jnp.sum(exchange(small, ("a", "zl")), axis=0)
    small = small[: pairs + width // 128]
    sent_gain = jnp.broadcast_to(
        small[pairs:].astype(jnp.bfloat16)[None], (pairs, width // LANES, LANES)
    )
    sent_slots = jnp.concatenate([half[:, :64] for half in halves(small[:pairs])], axis=1)
    extra = jnp.concatenate([sent_gain, sent_slots[:, None]], axis=1)
    extra = jnp.pad(extra, ((0, 0), (0, 8 - extra.shape[1]), (0, 0)))
    parts = exchange(jnp.concatenate([grad, extra], axis=1), "zh")
    last_gain = spread_gain(draft_gain[width // 2 :])
    grad_weight, grad_gain, slots = on_chip(
        finish,
        (
            jax.ShapeDtypeStruct((slab, width), jnp.float32),
            jax.ShapeDtypeStruct((width // LANES, LANES), jnp.float32),
            jax.ShapeDtypeStruct((pairs, LANES), jnp.float32),
        ),
        pairs * slab * width,
        (2 * pairs + 4) * slab * width,
        *(parts, first_gain, last_gain),
    )
    grad_gain = grad_gain.reshape(width)
    slots = slots[:, : quads * CAP] + slots[:, 64 : 64 + quads * CAP]
    slots = slots.reshape(pairs, 2, 2, CAP).transpose(1, 0, 2, 3)
    return (grad_weight, grad_gain, slots.reshape(groups * CAP))


def solution(mesh):
    fine = Mesh(mesh.devices.reshape(2, 8, 2, 4, 2, 2), DP + MP)
    in_specs = (
        P(DP, MP),
        P(),
        P(MP, None),
        P(MP),
        P(DP, MP),
        P(DP, MP),
        P(DP, None),
        P(DP),
        P(DP, None),
    )
    out_specs = (P(DP, MP), P(MP), P(DP))

    return jax.shard_map(
        on_device, mesh=fine, in_specs=in_specs, out_specs=out_specs, check_vma=False
    )
```

```python
import math

import jax
import jax.numpy as jnp
from jax import lax
from jax.experimental import pallas as pl
from jax.experimental.pallas import tpu as pltpu
from jax.sharding import Mesh, PartitionSpec as P


VOCAB = 32000
LEN = 128
CAP = 10
EPSILON = 1e-05
DP = ("a", "zh", "zl")
MP = ("x", "b", "c")


def exchange(value, axes):
    return lax.all_to_all(value, axes, split_axis=0, concat_axis=0, tiled=True)


def spread(value, axes):
    copies = lax.axis_size(axes)
    return exchange(jnp.broadcast_to(value[None], (copies,) + value.shape), axes)


def halves(value):
    high = value.astype(jnp.bfloat16)
    low = (value - high.astype(jnp.float32)).astype(jnp.bfloat16)
    return high, low


def flipped(value, axes):
    sizes = [lax.axis_size(axis) for axis in axes]
    last = math.prod(sizes) - 1
    return lax.ppermute(value, axes, [(k, last - k) for k in range(last + 1)])


def teacher_block(target_weight, a, zl, slab, width):
    x, b, c = (lax.axis_index(axis) for axis in MP)
    half = 2 * width
    ours = x // 2 == a

    def piece(shift):
        column = 2 * ((x + shift) % 4) + jnp.where(ours, b, 1 - b)
        return lax.dynamic_slice(target_weight, (zl * slab, column * half), (slab, half))

    pieces = lax.optimization_barrier([piece(shift) for shift in range(4)])
    came = pieces[:1]
    for shift in (1, 2, 3):
        came.append(
            lax.ppermute(pieces[shift], "x", [(k, (k + shift) % 4) for k in range(4)])
        )
    odd = ours == (x % 2 == 1)
    kept = jnp.concatenate([jnp.where(ours, came[0], came[2]), jnp.where(odd, came[1], came[3])])
    sent = jnp.concatenate([jnp.where(ours, came[2], came[0]), jnp.where(odd, came[3], came[1])])
    parts = kept, flipped(sent, ("a", "b"))

    def halve(parts, mine, axis):
        half = parts[0].shape[1] // 2

        def side(which):
            return jnp.concatenate(
                [lax.dynamic_slice_in_dim(part, which * half, half, axis=1) for part in parts]
            )

        return side(mine), flipped(side(1 - mine), (axis,))

    parts = halve(parts, c, "c")
    return [part.reshape(4, slab, width) for part in parts], 4 * (x % 2) + 2 * b + c


LANES = 128


def project(place, own, across, beside, both, wd, kept, came, gains, side, out):
    slab = wd.shape[1]
    mine = (out.shape[1] - side.shape[1]) // 4
    here = place[0]
    draft_gain, target_gain = gains[0:1], gains[1:2]
    for pair in range(4):
        merged = []
        for k in (2 * pair, 2 * pair + 1):
            away = here ^ k
            at = away // 2 % 2 * 2 + away // 4
            parts = kept[at], came[at]
            wt = jnp.where(away % 2 == 1, parts[1].astype(jnp.float32), parts[0].astype(jnp.float32))
            merged.append(wd[k].astype(jnp.float32) * draft_gain - wt * target_gain)
        merged = jnp.concatenate(merged).astype(jnp.bfloat16)
        for quad, block in enumerate((own, across, beside, both)):
            value = lax.dot_general(
                block[: 4 * mine],
                merged,
                (((1,), (1,)), ((), ())),
                preferred_element_type=jnp.float32,
            )
            out[4 * quad : 4 * quad + 4, pair * mine : (pair + 1) * mine] = value.astype(
                jnp.bfloat16
            ).reshape(4, mine, 2 * slab)
    out[:, 4 * mine :] = side[...]


def backward(got, own, across, beside, both, wd, out, gain):
    _, slab, width = wd.shape
    mine = slab
    total = jnp.zeros((1, width), jnp.float32)
    for chunk in range(4):
        grad = jnp.zeros((LANES, width), jnp.float32)
        for quad, block in enumerate((own, across, beside, both)):
            slope = got[4 * quad : 4 * quad + 4, chunk * mine : (chunk + 1) * mine]
            grad += lax.dot_general(
                slope.reshape(4 * mine, LANES),
                block[: 4 * mine],
                (((0,), (0,)), ((), ())),
                preferred_element_type=jnp.float32,
            )
        for k in range(2):
            rows = grad[k * slab : (k + 1) * slab]
            total += jnp.sum(rows * wd[2 * chunk + k].astype(jnp.float32), axis=0, keepdims=True)
            for part in range(width // LANES):
                out[2 * chunk + k, part * slab : (part + 1) * slab] = rows[
                    :, part * LANES : (part + 1) * LANES
                ].astype(jnp.bfloat16)
    gain[...] = total


def finish(parts, first_gain, last_gain, grad, gain, slots):
    pairs = parts.shape[0]
    slab, width = grad.shape
    chunks = width // LANES
    for chunk in range(chunks):
        total = parts[0, chunk * slab : (chunk + 1) * slab].astype(jnp.float32)
        for k in range(1, pairs):
            total += parts[k, chunk * slab : (chunk + 1) * slab].astype(jnp.float32)
        held = first_gain if chunk < chunks // 2 else last_gain
        grad[:, chunk * LANES : (chunk + 1) * LANES] = total * held[chunk % (chunks // 2), 0:1]
    total = parts[0, chunks * slab :].astype(jnp.float32)
    slots[0:1] = total[chunks : chunks + 1]
    for k in range(1, pairs):
        extra = parts[k, chunks * slab :].astype(jnp.float32)
        slots[k : k + 1] = extra[chunks : chunks + 1]
        total += extra
    gain[...] = total[:chunks]


def on_chip(kernel, out_shape, flops, moved, *args, scalars=0):
    space = [pl.BlockSpec(memory_space=pltpu.SMEM)] * scalars
    space += [pl.BlockSpec(memory_space=pltpu.VMEM)] * (len(args) - scalars)
    return pl.pallas_call(
        kernel,
        out_shape=out_shape,
        in_specs=space,
        out_specs=jax.tree.map(lambda _: pl.BlockSpec(memory_space=pltpu.VMEM), out_shape),
        cost_estimate=pl.CostEstimate(flops=flops, bytes_accessed=moved, transcendentals=0),
        compiler_params=pltpu.CompilerParams(vmem_limit_bytes=16 * 2**20),
    )(*args)


def spread_gain(part):
    part = part.reshape(-1, 1, LANES)
    return lax.optimization_barrier(jnp.broadcast_to(part, (part.shape[0], 8, LANES)))


def softmax_parts(logit_rows):
    values = logit_rows.astype(jnp.float32)
    highest = jnp.max(values, axis=1)
    shifted = values - highest[:, None]
    expsum = jnp.exp(shifted)
    return highest, jnp.sum(expsum, axis=1), jnp.sum(expsum * shifted, axis=1)


def on_device(
    hidden,
    target_gain,
    target_weight,
    draft_gain,
    draft_weight,
    logits,
    seq_lens,
    tool_mask,
    owners,
):
    rows, width = hidden.shape
    features = target_gain.shape[0]
    models = lax.axis_size(MP)
    groups = lax.axis_size(DP)
    pairs = lax.axis_size("zh")
    quads = groups // pairs
    slab = draft_weight.shape[0]
    columns = pairs * slab
    all_rows = quads * rows
    mine = all_rows // models
    a, zl = lax.axis_index("a"), lax.axis_index("zl")
    model = lax.axis_index(MP)
    scale = 1.0 / math.sqrt(rows * groups)

    index = jnp.arange(rows, dtype=jnp.int32)
    position = jnp.arange(LEN, dtype=jnp.int32)[None, :]
    reached = position < seq_lens[0][:, None] - 1
    valid = jnp.logical_and(reached, tool_mask.reshape(-1, LEN) == 1).reshape(rows)
    owner = owners[:, 0]
    earlier = jnp.logical_and(
        owner[:, None] == owner[None, :], index[:, None] < index[None, :]
    )
    rank = jnp.sum(earlier.astype(jnp.int32), axis=0)
    highest, total, moment = softmax_parts(logits)
    total_high, total_low = halves(total)
    moment_high, moment_low = halves(moment)
    facts = jnp.stack(
        [
            highest.astype(jnp.bfloat16),
            total_high,
            total_low,
            moment_high,
            moment_low,
            valid.astype(jnp.bfloat16),
            owner.astype(jnp.bfloat16),
            rank.astype(jnp.bfloat16),
        ]
    )
    kinds = facts.shape[0]

    wd = spread(draft_weight, "zh").reshape(columns, width)
    own = jnp.concatenate([hidden, jnp.pad(facts, ((0, 0), (0, width - rows)))], axis=0)
    across = flipped(own, ("a",))
    beside = flipped(own, ("zl",))
    both = flipped(across, ("zl",))
    blocks = (own, across, beside, both)
    facts_here = jnp.stack([block[rows:, :rows] for block in blocks])
    (kept, came), place = teacher_block(target_weight, a, zl, slab, width)

    gain_slice = lax.dynamic_slice_in_dim(target_gain, model * width, width)
    gains = jnp.stack([draft_gain, gain_slice])
    squares = []
    for block in blocks:
        squares.append(jnp.sum(block[:rows].astype(jnp.float32) ** 2, axis=1))
    squares = jnp.stack(halves(jnp.stack(squares))).reshape(2, models, mine)
    facts_here = facts_here.swapaxes(0, 1).reshape(kinds, models, mine)
    side = jnp.concatenate([facts_here, squares], axis=0).swapaxes(0, 1)
    side = side.reshape(models, (kinds + 2) * mine // LANES, LANES)
    side = jnp.pad(side, ((0, 0), (0, 8 - side.shape[1]), (0, 0)))
    held = columns // LANES * mine
    flops = 2 * all_rows * width * columns
    moved = 2 * (2 * all_rows * width + 2 * columns * width)
    wd = wd.reshape(pairs, slab, width)
    partial = on_chip(
        project,
        jax.ShapeDtypeStruct((models, held + 8, LANES), jnp.bfloat16),
        flops,
        moved,
        *(place.reshape(1), *blocks, wd, kept, came, gains, side),
        scalars=1,
    )
    got = exchange(partial, MP)
    first_gain = spread_gain(draft_gain[: width // 2])
    summed = jnp.sum(got[:, :held].astype(jnp.float32), axis=0).reshape(held // mine, mine, LANES)
    side = got[:, held : held + (kinds + 2) * mine // LANES]
    side = side.reshape(models, kinds + 2, mine).astype(jnp.float32)
    peaks = side[:, 0]
    totals = side[:, 1] + side[:, 2]
    moments = side[:, 3] + side[:, 4]
    peak = jnp.max(peaks, axis=0)
    below = peaks - peak
    factor = jnp.exp(below)
    total = jnp.sum(factor * totals, axis=0)
    moment = jnp.sum(factor * (moments + below * totals), axis=0)
    entropy = jnp.log(total) - moment / total
    weight = (side[0, 5] * entropy / math.log(VOCAB)).astype(jnp.bfloat16).astype(jnp.float32)
    square = jnp.sum(side[:, 8] + side[:, 9], axis=0)
    inverse = lax.rsqrt(square / features + EPSILON)
    error = summed * inverse[None, :, None]
    loss = 0.5 * weight * jnp.sum(error * error, axis=(0, 2)) * scale
    slope = (error * (weight * inverse * scale)[None, :, None]).astype(jnp.bfloat16)
    tail = jnp.concatenate(
        [jnp.stack(halves(loss)), side[0, 6:8].astype(jnp.bfloat16)], axis=0
    ).reshape(4 * mine // LANES, LANES)
    tail = jnp.pad(tail, ((0, 8 - tail.shape[0]), (0, 0)))
    got = spread(jnp.concatenate([slope.reshape(held, LANES), tail], axis=0), MP)
    tail = got[:, held : held + 4 * mine // LANES].reshape(models, 4, mine)
    tail = tail.swapaxes(0, 1).reshape(4, all_rows)
    grad, gain = on_chip(
        backward,
        (
            jax.ShapeDtypeStruct((pairs, width // LANES * slab, LANES), jnp.bfloat16),
            jax.ShapeDtypeStruct((1, width), jnp.float32),
        ),
        flops,
        moved,
        *(got, *blocks, wd),
    )

    named = tail[2][None, :] == jnp.arange(groups, dtype=jnp.bfloat16)[:, None]
    block = jnp.arange(all_rows, dtype=jnp.int32) // rows
    quad = 2 * (a ^ (block % 2)) + (zl ^ (block // 2))
    place = quad * CAP + tail[3].astype(jnp.int32)
    there = place[:, None] == jnp.arange(128, dtype=jnp.int32)[None, :]
    zero = jnp.zeros((), jnp.bfloat16)
    named = named.astype(jnp.bfloat16)
    slots = jnp.dot(
        jnp.concatenate([named, named], axis=1),
        jnp.concatenate(
            [jnp.where(there, tail[0][:, None], zero), jnp.where(there, tail[1][:, None], zero)],
            axis=0,
        ),
        preferred_element_type=jnp.float32,
    )
    slots = slots.reshape(2, pairs, 2, 128).transpose(0, 2, 1, 3).reshape(quads, pairs, 128)
    gain = jnp.broadcast_to(gain.reshape(1, width // 128, 128), (quads, width // 128, 128))
    small = jnp.concatenate([slots, gain, jnp.zeros((quads, 4, 128), jnp.float32)], axis=1)
    small = jnp.sum(exchange(small, ("a", "zl")), axis=0)
    small = small[: pairs + width // 128]
    sent_gain = jnp.broadcast_to(
        small[pairs:].astype(jnp.bfloat16)[None], (pairs, width // LANES, LANES)
    )
    sent_slots = jnp.concatenate([half[:, :64] for half in halves(small[:pairs])], axis=1)
    extra = jnp.concatenate([sent_gain, sent_slots[:, None]], axis=1)
    extra = jnp.pad(extra, ((0, 0), (0, 8 - extra.shape[1]), (0, 0)))
    parts = exchange(jnp.concatenate([grad, extra], axis=1), "zh")
    last_gain = spread_gain(draft_gain[width // 2 :])
    grad_weight, grad_gain, slots = on_chip(
        finish,
        (
            jax.ShapeDtypeStruct((slab, width), jnp.float32),
            jax.ShapeDtypeStruct((width // LANES, LANES), jnp.float32),
            jax.ShapeDtypeStruct((pairs, LANES), jnp.float32),
        ),
        pairs * slab * width,
        (2 * pairs + 4) * slab * width,
        *(parts, first_gain, last_gain),
    )
    grad_gain = grad_gain.reshape(width)
    slots = slots[:, : quads * CAP] + slots[:, 64 : 64 + quads * CAP]
    slots = slots.reshape(pairs, 2, 2, CAP).transpose(1, 0, 2, 3)
    return (grad_weight, grad_gain, slots.reshape(groups * CAP))


def solution(mesh):
    fine = Mesh(mesh.devices.reshape(2, 8, 2, 4, 2, 2), DP + MP)
    in_specs = (
        P(DP, MP),
        P(),
        P(MP, None),
        P(MP),
        P(DP, MP),
        P(DP, MP),
        P(DP, None),
        P(DP),
        P(DP, None),
    )
    out_specs = (P(DP, MP), P(MP), P(DP))

    return jax.shard_map(
        on_device, mesh=fine, in_specs=in_specs, out_specs=out_specs, check_vma=False
    )
```
